32 devices in a mesh: dp: 2 (over x), ctx: 16 (over z, y, core).
Axes of the slice: x: 2, y: 2, z: 4, core: 2. Of those that a mesh axis runs over, the one named last changes fastest.
Arguments:
- queries: bfloat16 [2, 2048, 1024], P('dp', 'ctx')
- keys: bfloat16 [2, 2048, 1024], P('dp', 'ctx')
- values: bfloat16 [2, 2048, 1024], P('dp', 'ctx'), may hold values from -6 to 6
- out_weight: bfloat16 [1024, 1024], P('dp'), may hold values from -0.1875 to 0.1875
- out_grad: bfloat16 [2, 2048, 1024], P('dp', 'ctx'), may hold values from -6 to 6
- key_blocks: int32 [2, 8, 16, 2], P('dp'), may hold values from 0 to 15, as said below
- block_counts: int32 [2, 8, 16], P('dp'), may hold values from 1 to 2, as said below
Outputs:
- output: bfloat16 [2, 2048, 1024], P('dp', 'ctx')
- grad_queries: bfloat16 [2, 2048, 1024], P('dp', 'ctx')
- grad_keys: bfloat16 [2, 2048, 1024], P('dp', 'ctx')
- grad_values: bfloat16 [2, 2048, 1024], P('dp', 'ctx')
- grad_weight: float32 [1024, 1024], P(('dp', 'ctx'))
The draws below stay inside these ranges and needn't reach their ends.
Inputs may be any that keep to these rules, and one draw needn't show every extreme that they name: For netlist b, head h and query block s, key_blocks[b, h, s, 0] is s and entries 1 to block_counts[b, h, s] - 1 are distinct blocks below s; later entries are block numbers that are not attended. block_counts[b, h, s] is at most s + 1; head 0's last block attends 2 blocks in every netlist.
All inputs are finite; a program needn't handle non-finite values.
Results may differ from the reference program's by a relative error of at most 0.02.
Values may be sent and summed in bfloat16 or wider, within the bound.
No kernel may reach another device: no remote copies, remote signals or barrier semaphores. Data moves between devices by JAX's collectives and lax.ppermute only.
A program may use at most 128 MiB of HBM per device.

```python
import jax
import jax.numpy as jnp
from jax import lax

HEADS = 8
HEAD_SIZE = 128
DOUT = 1024
BLOCK = 128
SLOTS = 2
BATCH = 2
NBLK = 16
SEQ = 2048
DIN = 1024
N_CTX = 16


def mask_tables(key):
    base = jax.random.fold_in(key, 7)
    key_dense, key_count, key_order = jax.random.split(base, 3)
    density = jax.random.randint(key_dense, (BATCH, HEADS, 1), 1, SLOTS + 1)
    drawn = jax.random.randint(key_count, (BATCH, HEADS, NBLK), 1, SLOTS + 1)
    counts = jnp.minimum(jnp.minimum(drawn, density), jnp.arange(NBLK)[None, None, :] + 1)
    counts = counts.at[:, 0, NBLK - 1].set(SLOTS)
    ranks = jax.random.randint(key_order, (BATCH, HEADS, NBLK, NBLK), 0, 2 ** 20)
    column = jnp.arange(NBLK)[None, :]
    rowpos = jnp.arange(NBLK)[:, None]
    priority = ranks * NBLK + column
    priority = jnp.where(column == rowpos, 2 ** 30, jnp.where(column < rowpos, priority, -1 - column))
    _, chosen = lax.top_k(priority, SLOTS)
    return (chosen.astype(jnp.int32), counts.astype(jnp.int32))


def draw_key_blocks(key, part):
    return mask_tables(key)[0]


def draw_block_counts(key, part):
    return mask_tables(key)[1]


def attention_inputs(key):
    base = jax.random.fold_in(key, 11)
    key_q, key_k = jax.random.split(base)
    query_raw = jax.random.normal(key_q, (BATCH, SEQ, HEADS, HEAD_SIZE), jnp.float32)
    key_raw = jax.random.normal(key_k, (BATCH, SEQ, HEADS, HEAD_SIZE), jnp.float32)
    query_raw = jnp.clip(query_raw, -6.0, 6.0)
    key_raw = jnp.clip(key_raw, -6.0, 6.0)
    return (query_raw.reshape(BATCH, SEQ, DIN).astype(jnp.bfloat16), key_raw.reshape(BATCH, SEQ, DIN).astype(jnp.bfloat16))


def draw_queries(key, part):
    return attention_inputs(key)[0]


def draw_keys(key, part):
    return attention_inputs(key)[1]


def level_of(rng, dims, pieces, smallest, largest):
    def one(dim, shards_of):
        heights = jax.random.uniform(jax.random.fold_in(jax.random.fold_in(rng, 6), dim), (shards_of,), jnp.float32, smallest / len(pieces), largest / len(pieces))
        return jnp.repeat(jnp.exp(heights), dims[dim] // shards_of).reshape((-1,) + (1,) * (len(dims) - dim - 1))

    loudness = one(*pieces[0])
    for cut in pieces[1:]:
        loudness = loudness * one(*cut)
    return loudness


def noise(key, extent, width, reach, shards=(), held_as=jnp.bfloat16):
    entries = jax.random.normal(key, extent, jnp.float32) * width
    if len(shards) > 0:
        entries = level_of(key, extent, shards, -0.22, 0.18) * entries
    return jnp.clip(entries, min=-reach, max=reach).astype(held_as)


def setup_inputs(seed: int = 0) -> dict:
    seeds = jax.random.split(jax.random.key(seed), 8)
    queries = draw_queries(jax.random.fold_in(seeds[7], 71), 0)
    keys = draw_keys(jax.random.fold_in(seeds[7], 71), 0)
    values = noise(seeds[2], (BATCH, SEQ, DIN), 1.0, 6.0, ((0, 2), (1, 16)))
    out_weight = noise(seeds[3], (DIN, DOUT), DIN ** -0.5, 0.1875, ((0, 2),))
    out_grad = noise(seeds[4], (BATCH, SEQ, DOUT), 1.0, 6.0, ((0, 2), (1, 16)))
    key_blocks = draw_key_blocks(jax.random.fold_in(seeds[7], 71), 0)
    block_counts = draw_block_counts(jax.random.fold_in(seeds[7], 71), 0)
    return dict(queries=queries, keys=keys, values=values, out_weight=out_weight, out_grad=out_grad, key_blocks=key_blocks, block_counts=block_counts)


def attend_head(qh, kh, vh, doh, idx, cnt):
    score_scale = HEAD_SIZE ** -0.5
    group = N_CTX // HEADS
    rows_sub = BLOCK // group
    valid_entries = jnp.arange(SLOTS)[:, None] < cnt[None, :]
    query_rows = qh.astype(jnp.float32)
    output_grad_rows = doh.astype(jnp.float32)

    def scores_at(slot_index):
        selected_entries = kh[idx[:, slot_index]].astype(jnp.float32)
        return jnp.einsum('lqo,lco->lqc', query_rows, selected_entries) * score_scale

    logit_scores = lax.map(scores_at, jnp.arange(SLOTS))
    valid_mask = valid_entries[:, :, None, None]
    highest_choice = jnp.max(jnp.where(valid_mask, logit_scores, -jnp.inf), axis=(0, 3), keepdims=True)
    exponent_values = jnp.where(valid_mask, jnp.exp(logit_scores - highest_choice), 0.0)
    probs = exponent_values / jnp.sum(exponent_values, axis=(0, 3), keepdims=True)
    block_probabilities = lax.optimization_barrier(probs.astype(jnp.bfloat16))

    def out_step(running_sum, slot_index):
        selected_entries = vh[idx[:, slot_index]].astype(jnp.float32)
        return running_sum + jnp.einsum('zij,zjh->zih', block_probabilities[slot_index].astype(jnp.float32), selected_entries), None

    running_sum, _ = lax.scan(out_step, jnp.zeros((NBLK, BLOCK, HEAD_SIZE), jnp.float32), jnp.arange(SLOTS))
    attn = lax.optimization_barrier(running_sum.astype(jnp.bfloat16))
    delta = jnp.sum(output_grad_rows * attn.astype(jnp.float32), axis=-1)

    def back_step(carry, slot_index):
        query_gradient, key_acc, val_acc = carry
        picked_keys = kh[idx[:, slot_index]].astype(jnp.float32)
        picked_values = vh[idx[:, slot_index]].astype(jnp.float32)
        prob_gradient = jnp.einsum('lqo,lco->lqc', output_grad_rows, picked_values)
        score_gradient = lax.optimization_barrier((probs[slot_index] * (prob_gradient - delta[..., None])).astype(jnp.bfloat16))
        score_gradient_rows = score_gradient.astype(jnp.float32)
        query_gradient = query_gradient + jnp.einsum('zij,zjh->zih', score_gradient_rows, picked_keys)
        dsg = score_gradient_rows.reshape(NBLK, group, rows_sub, BLOCK)
        qgr = query_rows.reshape(NBLK, group, rows_sub, HEAD_SIZE)
        key_acc = key_acc.at[:, idx[:, slot_index]].add(jnp.einsum('bgrk,bgrd->gbkd', dsg, qgr))
        pgr = block_probabilities[slot_index].astype(jnp.float32).reshape(NBLK, group, rows_sub, BLOCK)
        dgr = output_grad_rows.reshape(NBLK, group, rows_sub, HEAD_SIZE)
        val_acc = val_acc.at[:, idx[:, slot_index]].add(jnp.einsum('bgrk,bgrd->gbkd', pgr, dgr))
        return (query_gradient, key_acc, val_acc), None

    start = (jnp.zeros((NBLK, BLOCK, HEAD_SIZE), jnp.float32),
             jnp.zeros((group, NBLK, BLOCK, HEAD_SIZE), jnp.float32),
             jnp.zeros((group, NBLK, BLOCK, HEAD_SIZE), jnp.float32))
    (query_gradient, key_acc, val_acc), _ = lax.scan(back_step, start, jnp.arange(SLOTS))
    query_gradient = (query_gradient * score_scale).astype(jnp.bfloat16)
    key_parts = (key_acc * score_scale).astype(jnp.bfloat16).astype(jnp.float32)
    val_parts = val_acc.astype(jnp.bfloat16).astype(jnp.float32)
    grad_k = jnp.sum(key_parts, axis=0).astype(jnp.bfloat16)
    grad_v = jnp.sum(val_parts, axis=0).astype(jnp.bfloat16)
    return attn, query_gradient, grad_k, grad_v


def to_heads(x):
    return x.reshape(BATCH, NBLK, BLOCK, HEADS, HEAD_SIZE).transpose(0, 3, 1, 2, 4).reshape(BATCH * HEADS, NBLK, BLOCK, HEAD_SIZE)


def from_heads(x):
    return x.reshape(BATCH, HEADS, NBLK, BLOCK, HEAD_SIZE).transpose(0, 2, 3, 1, 4).reshape(BATCH, SEQ, DIN)


def reference(queries, keys, values, out_weight, out_grad, key_blocks, block_counts):
    grad_flat = out_grad.reshape(BATCH * SEQ, DOUT)
    d_out = jnp.dot(grad_flat, out_weight.T, preferred_element_type=jnp.float32).astype(jnp.bfloat16)
    d_out = d_out.reshape(BATCH, SEQ, DIN)
    stacked = (to_heads(queries), to_heads(keys), to_heads(values), to_heads(d_out),
               key_blocks.reshape(BATCH * HEADS, NBLK, SLOTS).astype(jnp.int32),
               block_counts.reshape(BATCH * HEADS, NBLK).astype(jnp.int32))
    attn, query_gradient, grad_k, grad_v = lax.map(lambda item: attend_head(*item), stacked)
    attn_flat = from_heads(attn).reshape(BATCH * SEQ, DIN)
    output = jnp.dot(attn_flat, out_weight, preferred_element_type=jnp.float32).astype(jnp.bfloat16)
    grad_weight = jnp.dot(attn_flat.T, grad_flat, preferred_element_type=jnp.float32)
    return (output.reshape(BATCH, SEQ, DOUT), from_heads(query_gradient), from_heads(grad_k),
            from_heads(grad_v), grad_weight)
```

```python
import functools

import jax
import jax.numpy as jnp
from jax import lax
from jax.experimental import pallas as pl
from jax.experimental.pallas import tpu as pltpu
from jax.sharding import PartitionSpec as P

HEADS = 8
HEAD_SIZE = 128
BLOCK = 128
SCALE = HEAD_SIZE ** (-0.5)
F32 = jnp.float32
BF16 = jnp.bfloat16
VMEM = pl.BlockSpec(memory_space=pltpu.VMEM)
SMEM = pl.BlockSpec(memory_space=pltpu.SMEM)
NN = (((1,), (0,)), ((), ()))
NT = (((1,), (1,)), ((), ()))
TN = (((0,), (0,)), ((), ()))


def dot(a, b, dims):
    return lax.dot_general(a, b, dims, preferred_element_type=F32)


def call(body, outs, scratch=(), n_smem=0, n_vmem=0, flops=0, moved=0, exps=0, name=None):
    many = isinstance(outs, (list, tuple))
    return pl.pallas_call(
        body,
        out_shape=outs,
        in_specs=[SMEM] * n_smem + [VMEM] * n_vmem,
        out_specs=[VMEM] * len(outs) if many else VMEM,
        scratch_shapes=list(scratch),
        compiler_params=pltpu.CompilerParams(vmem_limit_bytes=32 * 2**20),
        cost_estimate=pl.CostEstimate(flops=flops, bytes_accessed=moved, transcendentals=exps),
        name=name,
    )


def shape(dims, dtype=BF16):
    return jax.ShapeDtypeStruct(dims, dtype)


def head_lanes(h):
    return slice(h * HEAD_SIZE, (h + 1) * HEAD_SIZE)


def pack_body(q_ref, k_ref, v_ref, send_ref):
    for h in range(HEADS):
        for part, ref in enumerate((q_ref, k_ref, v_ref)):
            send_ref[h, part * BLOCK : (part + 1) * BLOCK, :] = ref[0, :, head_lanes(h)]


def unpack_body(recv_ref, q_ref, k_ref, v_ref):
    for h in range(HEADS):
        for part, ref in enumerate((q_ref, k_ref, v_ref)):
            ref[0, :, head_lanes(h)] = recv_ref[h, part * BLOCK : (part + 1) * BLOCK, :]


def d_out_body(ids_ref, grad_ref, near_ref, far_ref, d_out_ref):
    half = HEADS // 2
    for side, ref in enumerate((near_ref, far_ref)):
        for i in range(half):
            d_out_ref[(ids_ref[2] ^ side) * half + i] = dot(
                grad_ref[0], ref[i * HEAD_SIZE : (i + 1) * HEAD_SIZE, :], NT
            ).astype(BF16)


def output_body(ids_ref, *refs):
    *attn_refs, near_ref, far_ref, out_ref = refs
    half = HEADS // 2
    total = jnp.zeros(out_ref.shape[1:], F32)
    for side, ref in enumerate((near_ref, far_ref)):
        for i in range(half):
            total += dot(
                attn_refs[0][(ids_ref[2] ^ side) * half + i, BLOCK:, :],
                ref[i * HEAD_SIZE : (i + 1) * HEAD_SIZE, :],
                NN,
            )
    out_ref[0] = total.astype(BF16)


def gather_kv(own_ref, other_ref, kv_ref):
    kv_ref[0] = own_ref[:, BLOCK:, :]
    for r in range(other_ref.shape[0]):
        kv_ref[r + 1] = other_ref[r]


def second_block(ids_ref, kb_ref, j, group):
    block = kb_ref[0, ids_ref[0], j * group + ids_ref[1], 1]
    return (block % group) ^ ids_ref[1], block // group


def forward_body(group, ids_ref, kb_ref, cnt_ref, own_ref, other_ref, d_out_ref, send_ref, probs_ref, kv_ref):
    gather_kv(own_ref, other_ref, kv_ref)
    for h in range(HEADS):
        send_ref[h, :BLOCK, :] = d_out_ref[h]
    for j in range(HEADS):
        r, jb = second_block(ids_ref, kb_ref, j, group)
        both = cnt_ref[0, ids_ref[0], j * group + ids_ref[1]] > 1
        q = own_ref[j, :BLOCK, :]
        s0 = dot(q, kv_ref[0, j, :BLOCK, :], NT) * SCALE
        s1 = dot(q, kv_ref[r, jb, :BLOCK, :], NT) * SCALE
        s1 = jnp.where(both, s1, -jnp.inf)
        top = jnp.max(jnp.maximum(s0, s1), axis=-1, keepdims=True)
        e0 = jnp.exp(s0 - top)
        e1 = jnp.exp(s1 - top)
        inverse = 1.0 / jnp.sum(e0 + e1, axis=-1, keepdims=True)
        p0 = e0 * inverse
        p1 = e1 * inverse
        probs_ref[j, :, :BLOCK] = p0
        probs_ref[j, :, BLOCK:] = p1
        send_ref[j, BLOCK:, :] = (
            dot(p0.astype(BF16), kv_ref[0, j, BLOCK:, :], NN)
            + dot(p1.astype(BF16), kv_ref[r, jb, BLOCK:, :], NN)
        ).astype(BF16)


def backward_body(
    group, ids_ref, kb_ref, own_ref, other_ref, sent_ref, recv_ref, probs_ref,
    dq_ref, near_ref, far_ref, kv_ref, acc_ref,
):
    gather_kv(own_ref, other_ref, kv_ref)
    for r in range(1, group):
        acc_ref[r] = jnp.zeros(acc_ref.shape[1:], F32)
    second = []
    for j in range(HEADS):
        r, jb = second_block(ids_ref, kb_ref, j, group)
        q = own_ref[j, :BLOCK, :]
        do = recv_ref[j, :BLOCK, :]
        delta = jnp.sum(
            do.astype(F32) * sent_ref[j, BLOCK:, :].astype(F32), axis=-1, keepdims=True
        )
        p0 = probs_ref[j, :, :BLOCK]
        p1 = probs_ref[j, :, BLOCK:]
        ds0 = (p0 * (dot(do, kv_ref[0, j, BLOCK:, :], NT) - delta)).astype(BF16)
        ds1 = (p1 * (dot(do, kv_ref[r, jb, BLOCK:, :], NT) - delta)).astype(BF16)
        dq_ref[j] = (
            (dot(ds0, kv_ref[0, j, :BLOCK, :], NN) + dot(ds1, kv_ref[r, jb, :BLOCK, :], NN)) * SCALE
        ).astype(BF16)
        acc_ref[0, j, :BLOCK, :] = dot(ds0, q, TN)
        acc_ref[0, j, BLOCK:, :] = dot(p0.astype(BF16), do, TN)
        second.append((r, jb, dot(ds1, q, TN), dot(p1.astype(BF16), do, TN)))
    for r, jb, dk, dv in second:
        acc_ref[r, jb, :BLOCK, :] += dk
        acc_ref[r, jb, BLOCK:, :] += dv
    near_ref[:, :BLOCK, :] = acc_ref[0, :, :BLOCK, :] * SCALE
    near_ref[:, BLOCK:, :] = acc_ref[0, :, BLOCK:, :]
    for r in range(1, group):
        far_ref[r - 1, :, :BLOCK, :] = (acc_ref[r, :, :BLOCK, :] * SCALE).astype(BF16)
        far_ref[r - 1, :, BLOCK:, :] = acc_ref[r, :, BLOCK:, :].astype(BF16)


def combine_body(dq_ref, near_ref, arrived_ref, send_ref):
    send_ref[:, :BLOCK, :] = dq_ref[...]
    total = near_ref[...]
    for r in range(arrived_ref.shape[0]):
        total += arrived_ref[r].astype(F32)
    send_ref[:, BLOCK:, :] = total.astype(BF16)


def grad_weight_body(
    ids_ref, mine_ref, pair_ref, grad_ref, pair_grad_ref,
    a_keep_ref, a_send_ref, b_keep_ref, b_send_ref, rows_ref, both_ref,
):
    rows_ref[:BLOCK] = grad_ref[0]
    rows_ref[BLOCK:] = pair_grad_ref[0]
    d, z, y, c = ids_ref[2], ids_ref[3], ids_ref[4], ids_ref[5]
    for zr in range(4):
        for dr in range(2):
            h = (dr ^ d) * 4 + (zr ^ z)
            attn = jnp.concatenate([mine_ref[h, BLOCK:, :], pair_ref[h, BLOCK:, :]], axis=0)
            slot = zr * 2 + dr
            both_ref[slot] = dot(attn, rows_ref[...], TN)
            for yr in range(2):
                first = pl.multiple_of((yr ^ y) * 64 + c * 32, 32)
                piece = both_ref[slot, pl.ds(first, 32), :].astype(BF16)
                if zr < 2:
                    (a_send_ref if dr else a_keep_ref)[zr, yr] = piece
                else:
                    (b_send_ref if yr else b_keep_ref)[dr, zr - 2] = piece


def ctx_swap(x, mask):
    n = lax.axis_size("ctx")
    return lax.ppermute(x, "ctx", [(i, i ^ mask) for i in range(n)])


def dp_swap(x):
    return lax.ppermute(x, "dp", [(0, 1), (1, 0)])


def members(x, group):
    return jnp.stack([ctx_swap(x, r) for r in range(1, group)])


def reduce_small_mesh(ids, back, out_grad):
    columns = out_grad.shape[-1]
    pair = ctx_swap(back, 1)
    pair_grad = ctx_swap(out_grad, 1)
    piece = shape((2, 2, 32, columns))
    a_keep, a_send, b_keep, b_send = call(
        grad_weight_body,
        [piece] * 4,
        scratch=[
            pltpu.VMEM((2 * BLOCK, columns), BF16),
            pltpu.VMEM((HEADS, HEAD_SIZE, columns), F32),
        ],
        n_smem=1, n_vmem=4, flops=2**29, moved=3 * 2**20, name="grad_weight",
    )(ids, back, pair, out_grad, pair_grad)
    a = a_keep.astype(F32) + dp_swap(a_send).astype(F32)
    b = b_keep.astype(F32) + ctx_swap(b_send, 2).astype(F32)
    a = a[:, 0] + ctx_swap(a[:, 1].astype(BF16), 2).astype(F32)
    b = b[0] + dp_swap(b[1].astype(BF16)).astype(F32)
    return (
        a[0]
        + ctx_swap(a[1].astype(BF16), 4).astype(F32)
        + ctx_swap(b[0].astype(BF16), 8).astype(F32)
        + ctx_swap(b[1].astype(BF16), 12).astype(F32)
    )


def local(queries, keys, values, out_weight, out_grad, key_blocks, block_counts):
    ctx_count = lax.axis_size("ctx")
    dp_count = lax.axis_size("dp")
    group = ctx_count // HEADS
    position = lax.axis_index("ctx")
    small = dp_count == 2 and ctx_count == 16
    rank = lax.axis_index("dp") if dp_count == 2 else 0
    ids = jnp.stack(
        [position // group, position % group, rank, position >> 2, position >> 1 & 1, position & 1]
    ).astype(jnp.int32)
    columns = out_grad.shape[-1]
    peers = [[j * group + m for j in range(HEADS)] for m in range(group)]

    def exchange(x):
        return lax.all_to_all(x, "ctx", 0, 0, tiled=True, axis_index_groups=peers)

    if dp_count == 2:
        near, far = out_weight, dp_swap(out_weight)
    else:
        near, far = jnp.split(lax.all_gather(out_weight, "dp", axis=0, tiled=True), 2)

    sent = call(
        pack_body, shape((HEADS, 3 * BLOCK, HEAD_SIZE)), n_vmem=3, moved=3 * 2**19, name="pack"
    )(queries, keys, values)
    own = exchange(sent)
    d_out = call(
        d_out_body, shape((HEADS, BLOCK, HEAD_SIZE)), n_smem=1, n_vmem=3,
        flops=2**28, moved=3 * 2**20, name="d_out",
    )(ids, out_grad, near, far)
    other = members(own[:, BLOCK:, :], group)
    kv_scratch = pltpu.VMEM((group, HEADS, 2 * BLOCK, HEAD_SIZE), BF16)
    send, probs = call(
        functools.partial(forward_body, group),
        [shape((HEADS, 2 * BLOCK, HEAD_SIZE)), shape((HEADS, BLOCK, 2 * BLOCK), F32)],
        scratch=[kv_scratch], n_smem=3, n_vmem=3,
        flops=2**27, moved=3 * 2**20, exps=2**18, name="forward",
    )(ids, key_blocks, block_counts, own, other, d_out)
    back = exchange(send)
    dq, near_kv, far_kv = call(
        functools.partial(backward_body, group),
        [
            shape((HEADS, BLOCK, HEAD_SIZE)),
            shape((HEADS, 2 * BLOCK, HEAD_SIZE), F32),
            shape((group - 1, HEADS, 2 * BLOCK, HEAD_SIZE)),
        ],
        scratch=[kv_scratch, pltpu.VMEM((group, HEADS, 2 * BLOCK, HEAD_SIZE), F32)],
        n_smem=2, n_vmem=5, flops=2**28, moved=2**22, name="backward",
    )(ids, key_blocks, own, other, send, back, probs)
    arrived = jnp.stack([ctx_swap(far_kv[r - 1], r) for r in range(1, group)])
    grads = exchange(
        call(
            combine_body, shape((HEADS, 3 * BLOCK, HEAD_SIZE)), n_vmem=3, moved=3 * 2**20, name="combine"
        )(dq, near_kv, arrived)
    )
    tokens = shape((1, BLOCK, HEADS * HEAD_SIZE))
    grad_queries, grad_keys, grad_values = call(
        unpack_body, [tokens] * 3, n_vmem=1, moved=3 * 2**19, name="unpack"
    )(grads)
    if small:
        grad_weight = reduce_small_mesh(ids, back, out_grad)
    else:
        attn = back[:, BLOCK:, :].transpose(1, 0, 2).reshape(BLOCK, HEADS * HEAD_SIZE)
        grad_weight = lax.psum_scatter(
            dot(attn, out_grad[0], TN), ("dp", "ctx"), scatter_dimension=0, tiled=True
        )
    output = call(
        output_body, shape((1, BLOCK, columns)), n_smem=1, n_vmem=3,
        flops=2**28, moved=3 * 2**20, name="output",
    )(ids, back, near, far)
    return (output, grad_queries, grad_keys, grad_values, grad_weight)


def solution(mesh):
    tokens = P("dp", "ctx", None)
    return jax.shard_map(
        local,
        mesh=mesh,
        in_specs=(
            tokens, tokens, tokens, P("dp", None), tokens,
            P("dp", None, None, None), P("dp", None, None),
        ),
        out_specs=(tokens, tokens, tokens, tokens, P(("dp", "ctx"), None)),
        check_vma=False,
    )
```

```python
import functools

import jax
import jax.numpy as jnp
from jax import lax
from jax.experimental import pallas as pl
from jax.experimental.pallas import tpu as pltpu
from jax.sharding import PartitionSpec as P

HEADS = 8
HEAD_SIZE = 128
BLOCK = 128
SCALE = HEAD_SIZE ** (-0.5)
F32 = jnp.float32
BF16 = jnp.bfloat16
VMEM = pl.BlockSpec(memory_space=pltpu.VMEM)
HBM = pl.BlockSpec(memory_space=pltpu.HBM)
SMEM = pl.BlockSpec(memory_space=pltpu.SMEM)
NN = (((1,), (0,)), ((), ()))
NT = (((1,), (1,)), ((), ()))
TN = (((0,), (0,)), ((), ()))


def dot(a, b, dims):
    return lax.dot_general(a, b, dims, preferred_element_type=F32)


def call(body, outs, scratch=(), n_smem=0, n_vmem=0, n_hbm=0, out_specs=None, vmem=16, alias=None, flops=0, name=None):
    many = isinstance(outs, (list, tuple))
    return pl.pallas_call(
        body,
        out_shape=outs,
        in_specs=[SMEM] * n_smem + [VMEM] * n_vmem + [HBM] * n_hbm,
        out_specs=out_specs or ([VMEM] * len(outs) if many else VMEM),
        scratch_shapes=list(scratch),
        input_output_aliases=alias or {},
        compiler_params=pltpu.CompilerParams(vmem_limit_bytes=vmem * 2**20),
        cost_estimate=pl.CostEstimate(flops=flops, bytes_accessed=0, transcendentals=0),
        name=name,
    )


def shape(dims, dtype=BF16):
    return jax.ShapeDtypeStruct(dims, dtype)


def head_lanes(h):
    return slice(h * HEAD_SIZE, (h + 1) * HEAD_SIZE)


def pack_body(q_ref, k_ref, v_ref, send_ref, wide_ref, tall_ref, in_sems, out_sems):
    inward = [
        pltpu.make_async_copy(ref.at[0], wide_ref.at[part], in_sems.at[part])
        for part, ref in enumerate((q_ref, k_ref, v_ref))
    ]
    outward = [
        pltpu.make_async_copy(
            tall_ref.at[part], send_ref.at[:, pl.ds(part * BLOCK, BLOCK), :], out_sems.at[part]
        )
        for part in range(3)
    ]
    for copy in inward:
        copy.start()
    for part in range(3):
        inward[part].wait()
        for h in range(HEADS):
            tall_ref[part, h] = wide_ref[part, :, head_lanes(h)]
        outward[part].start()
    for copy in outward:
        copy.wait()


def pack(*arrays):
    width = arrays[0].shape[-1]
    return pl.pallas_call(
        pack_body,
        out_shape=shape((HEADS, 3 * BLOCK, HEAD_SIZE)),
        in_specs=[HBM] * 3,
        out_specs=HBM,
        scratch_shapes=[
            pltpu.VMEM((3, BLOCK, width), BF16),
            pltpu.VMEM((3, HEADS, BLOCK, HEAD_SIZE), BF16),
            pltpu.SemaphoreType.DMA((3,)),
            pltpu.SemaphoreType.DMA((3,)),
        ],
        compiler_params=pltpu.CompilerParams(vmem_limit_bytes=60 * 2**20),
        cost_estimate=pl.CostEstimate(flops=2**35, bytes_accessed=0, transcendentals=0),
        name="pack",
    )(*arrays)


def unpack_body(recv_ref, q_ref, k_ref, v_ref):
    for part, ref in enumerate((q_ref, k_ref, v_ref)):
        for h in range(HEADS):
            ref[0, :, head_lanes(h)] = recv_ref[h, part * BLOCK : (part + 1) * BLOCK, :]


def weight_rows(ids_ref, refs, place):
    half, quarter = HEADS // 2, HEADS // 4
    i = place % quarter
    near_ref, *far_refs = refs
    if place < half:
        return ids_ref[2] * half + place, near_ref[place * HEAD_SIZE : (place + 1) * HEAD_SIZE, :]
    part = (place - half) // quarter
    h = (ids_ref[2] ^ 1) * half + (part ^ ids_ref[6]) * quarter + i
    return h, far_refs[part][i * HEAD_SIZE : (i + 1) * HEAD_SIZE, :]


def d_out_body(ids_ref, grad_ref, *refs):
    *weight_refs, send_ref, tile_ref, sem = refs
    for place in range(HEADS):
        h, weight = weight_rows(ids_ref, weight_refs, place)
        tile_ref[h] = dot(grad_ref[0], weight, NT).astype(BF16)
    copy = pltpu.make_async_copy(tile_ref, send_ref.at[:, pl.ds(0, BLOCK), :], sem)
    copy.start()
    copy.wait()


def output_body(ids_ref, back_ref, *refs):
    *weight_refs, out_ref = refs
    total = jnp.zeros(out_ref.shape[1:], F32)
    for place in range(HEADS):
        h, weight = weight_rows(ids_ref, weight_refs, place)
        total += dot(back_ref[h, BLOCK:, :], weight, TN)
    out_ref[0] = total.astype(BF16)


def second_block(ids_ref, kb_ref, j, group):
    block = kb_ref[0, ids_ref[0], j * group + ids_ref[1], 1]
    return (block % group) ^ ids_ref[1], block // group


def forward_body(group, ids_ref, kb_ref, cnt_ref, *refs):
    own_ref, *other_refs = refs[:group]
    _, send_ref, probs_ref, kv_ref, s_ref, p_ref, t_ref, sems = refs[group:]
    kv_ref[0] = own_ref[:, BLOCK:, :]
    for r, ref in enumerate(other_refs):
        kv_ref[r + 1] = ref[:, BLOCK:, :]
    picks = [second_block(ids_ref, kb_ref, j, group) for j in range(HEADS)]
    copies = []
    for j in range(HEADS):
        q = own_ref[j, :BLOCK, :]
        both = cnt_ref[0, ids_ref[0], j * group + ids_ref[1]] > 1
        s_ref[j, :, :BLOCK] = dot(q, kv_ref[0, j, :BLOCK, :], NT) * SCALE
        s1 = dot(q, kv_ref[picks[j][0], picks[j][1], :BLOCK, :], NT) * SCALE
        s_ref[j, :, BLOCK:] = jnp.where(both, s1, -jnp.inf)
    for j in range(HEADS):
        s = s_ref[j]
        e = jnp.exp(s - jnp.max(s, axis=-1, keepdims=True))
        p = e * (1.0 / jnp.sum(e, axis=-1, keepdims=True))
        p_ref[j] = p.astype(BF16)
    copies.append(pltpu.make_async_copy(p_ref, probs_ref, sems.at[0]))
    copies[-1].start()
    for j in range(HEADS):
        attn = dot(p_ref[j, :, :BLOCK], kv_ref[0, j, BLOCK:, :], NN) + dot(
            p_ref[j, :, BLOCK:], kv_ref[picks[j][0], picks[j][1], BLOCK:, :], NN
        )
        t_ref[j] = attn.T.astype(BF16)
    copies.append(pltpu.make_async_copy(t_ref, send_ref.at[:, pl.ds(BLOCK, BLOCK), :], sems.at[1]))
    copies[-1].start()
    for copy in copies:
        copy.wait()


def backward_body(group, ids_ref, kb_ref, back_ref, *refs):
    own_ref, *other_refs = refs[:group]
    probs_ref, dq_ref, near_ref, *far_refs = refs[group:-7]
    q_ref, kv_ref, p_ref, dp_ref, ds_ref, acc_ref, sems = refs[-7:]
    loads = [pltpu.make_async_copy(own_ref.at[:, pl.ds(BLOCK, 2 * BLOCK), :], kv_ref.at[0], sems.at[0])]
    for r, ref in enumerate(other_refs):
        loads.append(
            pltpu.make_async_copy(ref.at[:, pl.ds(BLOCK, 2 * BLOCK), :], kv_ref.at[r + 1], sems.at[r + 1])
        )
    loads.append(pltpu.make_async_copy(probs_ref, p_ref, sems.at[group]))
    loads.append(pltpu.make_async_copy(own_ref.at[:, pl.ds(0, BLOCK), :], q_ref, sems.at[group + 1]))
    for copy in loads:
        copy.start()
    picks = [second_block(ids_ref, kb_ref, j, group) for j in range(HEADS)]
    for r in range(1, group):
        acc_ref[r] = jnp.zeros(acc_ref.shape[1:], F32)
    for copy in loads[:group]:
        copy.wait()
    for j in range(HEADS):
        do = back_ref[j, :BLOCK, :]
        dp_ref[j, :, :BLOCK] = dot(do, kv_ref[0, j, BLOCK:, :], NT)
        dp_ref[j, :, BLOCK:] = dot(do, kv_ref[picks[j][0], picks[j][1], BLOCK:, :], NT)
    for copy in loads[group:]:
        copy.wait()
    for j in range(HEADS):
        p = p_ref[j].astype(F32)
        dp = dp_ref[j]
        delta = jnp.sum(p * dp, axis=-1, keepdims=True)
        ds_ref[j] = (p * (dp - delta)).astype(BF16)
    second = []
    for j in range(HEADS):
        dk = dot(ds_ref[j], q_ref[j], TN)
        dv = dot(p_ref[j], back_ref[j, :BLOCK, :], TN)
        acc_ref[0, j, :BLOCK, :] = dk[:BLOCK]
        acc_ref[0, j, BLOCK:, :] = dv[:BLOCK]
        dp_ref[j, :, :BLOCK] = dk[BLOCK:]
        dp_ref[j, :, BLOCK:] = dv[BLOCK:]
    for j in range(HEADS):
        r, jb = picks[j]
        acc_ref[r, jb, :BLOCK, :] += dp_ref[j, :, :BLOCK]
        acc_ref[r, jb, BLOCK:, :] += dp_ref[j, :, BLOCK:]
    for j in range(HEADS):
        dq_ref[j] = (
            (
                dot(ds_ref[j, :, :BLOCK], kv_ref[0, j, :BLOCK, :], NN)
                + dot(ds_ref[j, :, BLOCK:], kv_ref[picks[j][0], picks[j][1], :BLOCK, :], NN)
            )
            * SCALE
        ).astype(BF16)
    for r, ref in enumerate((near_ref, *far_refs)):
        ref[:, :BLOCK, :] = (acc_ref[r, :, :BLOCK, :] * SCALE).astype(BF16)
        ref[:, BLOCK:, :] = acc_ref[r, :, BLOCK:, :].astype(BF16)


def combine_body(dq_ref, near_ref, *refs):
    *arrived_refs, send_ref = refs
    send_ref[:, :BLOCK, :] = dq_ref[...]
    total = near_ref[...].astype(F32)
    for ref in arrived_refs:
        total += ref[...].astype(F32)
    send_ref[:, BLOCK:, :] = total.astype(BF16)


def feature_body(ids_ref, mine_ref, pair_ref, *out_refs):
    d, z, y, c = ids_ref[2], ids_ref[3], ids_ref[4], ids_ref[5]
    for yr, ref in enumerate(out_refs):
        first = pl.multiple_of(BLOCK + (yr ^ y) * 64 + c * 32, 32)
        for place in range(HEADS):
            h = ((place >> 2) ^ d) * 4 + ((place & 3) ^ z)
            rows = slice(place * 32, (place + 1) * 32)
            ref[rows, :BLOCK] = mine_ref[h, pl.ds(first, 32), :]
            ref[rows, BLOCK:] = pair_ref[h, pl.ds(first, 32), :]


def grad_weight_body(*refs):
    attn_refs, grad_refs = refs[:2], refs[2:6]
    keep_ref, send_ref, rows_ref, sems = refs[6:]
    loads = [
        pltpu.make_async_copy(ref.at[0], rows_ref.at[i], sems.at[i]) for i, ref in enumerate(grad_refs)
    ]
    for copy in loads:
        copy.start()
    for copy in loads:
        copy.wait()
    half = keep_ref.shape[0]
    for place, ref in ((1, send_ref), (0, keep_ref)):
        rows = slice(place * half, (place + 1) * half)
        total = jnp.zeros(ref.shape, F32)
        for i, attn_ref in enumerate(attn_refs):
            total += dot(attn_ref[rows, :BLOCK], rows_ref[i], NN)
            total += dot(attn_ref[rows, BLOCK:], rows_ref[i + 2], NN)
        ref[...] = total.astype(ref.dtype)


def ctx_swap(x, mask):
    n = lax.axis_size("ctx")
    return lax.ppermute(x, "ctx", [(i, i ^ mask) for i in range(n)])


def dp_swap(x):
    return lax.ppermute(x, "dp", [(0, 1), (1, 0)])


def together(*values):
    return lax.optimization_barrier(values)


def own_features(ids, back):
    return call(
        feature_body, [shape((HEADS * 32, 2 * BLOCK))] * 2, n_smem=1, n_vmem=2, name="features"
    )(ids, back, ctx_swap(back, 1))


def reduce_weight(features, rows):
    columns = rows[0].shape[-1]
    keep, send = call(
        grad_weight_body,
        [shape((4 * 32, columns), F32), shape((4 * 32, columns))],
        [pltpu.VMEM((4, BLOCK, columns), BF16), pltpu.SemaphoreType.DMA((4,))],
        n_vmem=2, n_hbm=4, vmem=16, flops=2**35, name="grad_weight",
    )(features[0], ctx_swap(features[1], 2), *rows)
    total = (keep + dp_swap(send).astype(F32)).reshape(4, 32, columns)
    parts = [ctx_swap(total[zr].astype(BF16), 4 * zr) for zr in range(1, 4)]
    return total[0] + sum(part.astype(F32) for part in parts)


def local(queries, keys, values, out_weight, out_grad, key_blocks, block_counts):
    ctx_count = lax.axis_size("ctx")
    dp_count = lax.axis_size("dp")
    group = ctx_count // HEADS
    position = lax.axis_index("ctx")
    small = dp_count == 2 and ctx_count == 16
    rank = lax.axis_index("dp") if dp_count == 2 else 0
    ids = jnp.stack(
        [position // group, position % group, rank, position >> 2, position >> 1 & 1, position & 1,
         position & 1 if dp_count == 2 else 0]
    ).astype(jnp.int32)
    columns = out_grad.shape[-1]
    peers = [[j * group + m for j in range(HEADS)] for m in range(group)]

    def exchange(x):
        return lax.all_to_all(x, "ctx", 0, 0, tiled=True, axis_index_groups=peers)

    if dp_count == 2:
        near, rows = out_weight, out_weight.shape[0] // 2
        half = dp_swap(lax.dynamic_slice_in_dim(near, (position & 1) * rows, rows, 0))
    if small:
        same, cross = [out_grad, ctx_swap(out_grad, 2)], [ctx_swap(out_grad, 1)]
        cross.append(ctx_swap(same[1], 1))
    if dp_count == 2:
        far = [half, ctx_swap(half, 1)]
    else:
        near, *far = jnp.split(
            lax.all_gather(out_weight, "dp", axis=0, tiled=True), (HEADS * 64, HEADS * 96)
        )

    own = exchange(pack(queries, keys, values))
    pair = shape((HEADS, 2 * BLOCK, HEAD_SIZE))
    tile = shape((HEADS, BLOCK, HEAD_SIZE))
    tile_scratch = pltpu.VMEM(tile.shape, BF16)
    score = (HEADS, BLOCK, 2 * BLOCK)
    if small:
        own, same[1], *rest = together(own, same[1], *cross, *far)
        cross, far = rest[:2], rest[2:]
    send = call(
        d_out_body, pair, [tile_scratch, pltpu.SemaphoreType.DMA],
        n_smem=1, n_vmem=4, out_specs=HBM, vmem=60, flops=2**33, name="d_out",
    )(ids, out_grad, near, *far)
    others = [ctx_swap(own, r) for r in range(1, group)]
    vmem = 16 if group == 2 else 40
    kv_scratch = pltpu.VMEM((group, HEADS, 2 * BLOCK, HEAD_SIZE), BF16)
    send, probs = call(
        functools.partial(forward_body, group),
        [pair, shape(score)],
        [kv_scratch, pltpu.VMEM(score, F32), pltpu.VMEM(score, BF16), tile_scratch, pltpu.SemaphoreType.DMA((2,))],
        n_smem=3, n_vmem=group, n_hbm=1, out_specs=[HBM] * 2, vmem=60, alias={3 + group: 0}, name="forward",
    )(ids, key_blocks, block_counts, own, *others, send)
    back = exchange(send)
    dq, near_kv, *far_kv = call(
        functools.partial(backward_body, group),
        [tile, pair] + [pair] * (group - 1),
        [
            tile_scratch, kv_scratch, pltpu.VMEM(score, BF16), pltpu.VMEM(score, F32), pltpu.VMEM(score, BF16),
            pltpu.VMEM((group, HEADS, 2 * BLOCK, HEAD_SIZE), F32), pltpu.SemaphoreType.DMA((group + 2,)),
        ],
        n_smem=2, n_vmem=1, n_hbm=group + 1, vmem=vmem, name="backward",
    )(ids, key_blocks, back, own, *others, probs)
    arrived = [ctx_swap(part, r + 1) for r, part in enumerate(far_kv)]
    if small:
        dq, *features = together(dq, *own_features(ids, back))
    grads = exchange(
        call(
            combine_body, shape((HEADS, 3 * BLOCK, HEAD_SIZE)), n_vmem=group + 1,
            vmem=vmem, flops=2**33, name="combine",
        )(dq, near_kv, *arrived)
    )
    tokens = shape((1, BLOCK, HEADS * HEAD_SIZE))
    grad_queries, grad_keys, grad_values = call(unpack_body, [tokens] * 3, n_vmem=1, name="unpack")(grads)
    if small:
        grad_weight = reduce_weight(features, same + cross)
    else:
        grad_weight = lax.psum_scatter(
            dot(back[:, BLOCK:, :].reshape(HEADS * HEAD_SIZE, BLOCK), out_grad[0], NN),
            ("dp", "ctx"), scatter_dimension=0, tiled=True,
        )
    output = call(
        output_body, shape((1, BLOCK, columns)), n_smem=1, n_vmem=4, vmem=60, name="output",
    )(ids, back, near, *far)
    return (output, grad_queries, grad_keys, grad_values, grad_weight)


def solution(mesh):
    tokens = P("dp", "ctx", None)
    return jax.shard_map(
        local,
        mesh=mesh,
        in_specs=(
            tokens, tokens, tokens, P("dp", None), tokens,
            P("dp", None, None, None), P("dp", None, None),
        ),
        out_specs=(tokens, tokens, tokens, tokens, P(("dp", "ctx"), None)),
        check_vma=False,
    )
```

```python
import functools

import jax
import jax.numpy as jnp
from jax import lax
from jax.experimental import pallas as pl
from jax.experimental.pallas import tpu as pltpu
from jax.sharding import PartitionSpec as P

HEADS = 8
HEAD_SIZE = 128
BLOCK = 128
SCALE = HEAD_SIZE ** (-0.5)
F32 = jnp.float32
BF16 = jnp.bfloat16
VMEM = pl.BlockSpec(memory_space=pltpu.VMEM)
HBM = pl.BlockSpec(memory_space=pltpu.HBM)
SMEM = pl.BlockSpec(memory_space=pltpu.SMEM)
NN = (((1,), (0,)), ((), ()))
NT = (((1,), (1,)), ((), ()))
TN = (((0,), (0,)), ((), ()))


def dot(a, b, dims):
    return lax.dot_general(a, b, dims, preferred_element_type=F32)


def call(body, outs, scratch=(), n_smem=0, n_vmem=0, n_hbm=0, out_specs=None, vmem=16, alias=None, flops=0, name=None):
    many = isinstance(outs, (list, tuple))
    return pl.pallas_call(
        body,
        out_shape=outs,
        in_specs=[SMEM] * n_smem + [VMEM] * n_vmem + [HBM] * n_hbm,
        out_specs=out_specs or ([VMEM] * len(outs) if many else VMEM),
        scratch_shapes=list(scratch),
        input_output_aliases=alias or {},
        compiler_params=pltpu.CompilerParams(vmem_limit_bytes=vmem * 2**20),
        cost_estimate=pl.CostEstimate(flops=flops, bytes_accessed=0, transcendentals=0),
        name=name,
    )


def shape(dims, dtype=BF16):
    return jax.ShapeDtypeStruct(dims, dtype)


def head_lanes(h):
    return slice(h * HEAD_SIZE, (h + 1) * HEAD_SIZE)


def pack_body(q_ref, k_ref, v_ref, send_ref, wide_ref, tall_ref, in_sems, out_sems):
    inward = [
        pltpu.make_async_copy(ref.at[0], wide_ref.at[part], in_sems.at[part])
        for part, ref in enumerate((q_ref, k_ref, v_ref))
    ]
    outward = [
        pltpu.make_async_copy(
            tall_ref.at[part], send_ref.at[:, pl.ds(part * BLOCK, BLOCK), :], out_sems.at[part]
        )
        for part in range(3)
    ]
    for copy in inward:
        copy.start()
    for part in range(3):
        inward[part].wait()
        for h in range(HEADS):
            tall_ref[part, h] = wide_ref[part, :, head_lanes(h)]
        outward[part].start()
    for copy in outward:
        copy.wait()


def pack(*arrays):
    width = arrays[0].shape[-1]
    return pl.pallas_call(
        pack_body,
        out_shape=shape((HEADS, 3 * BLOCK, HEAD_SIZE)),
        in_specs=[HBM] * 3,
        out_specs=HBM,
        scratch_shapes=[
            pltpu.VMEM((3, BLOCK, width), BF16),
            pltpu.VMEM((3, HEADS, BLOCK, HEAD_SIZE), BF16),
            pltpu.SemaphoreType.DMA((3,)),
            pltpu.SemaphoreType.DMA((3,)),
        ],
        compiler_params=pltpu.CompilerParams(vmem_limit_bytes=60 * 2**20),
        cost_estimate=pl.CostEstimate(flops=2**35, bytes_accessed=0, transcendentals=0),
        name="pack",
    )(*arrays)


def unpack_body(recv_ref, q_ref, k_ref, v_ref):
    for part, ref in enumerate((q_ref, k_ref, v_ref)):
        for h in range(HEADS):
            ref[0, :, head_lanes(h)] = recv_ref[h, part * BLOCK : (part + 1) * BLOCK, :]


def weight_rows(ids_ref, refs, place):
    half, quarter = HEADS // 2, HEADS // 4
    i = place % quarter
    near_ref, *far_refs = refs
    if place < half:
        return ids_ref[2] * half + place, near_ref[place * HEAD_SIZE : (place + 1) * HEAD_SIZE, :]
    part = (place - half) // quarter
    h = (ids_ref[2] ^ 1) * half + (part ^ ids_ref[6]) * quarter + i
    return h, far_refs[part][i * HEAD_SIZE : (i + 1) * HEAD_SIZE, :]


def d_out_body(ids_ref, grad_ref, *refs):
    *weight_refs, tile_ref = refs[: -HEADS - 1] + refs[-1:]
    piece_refs = refs[-HEADS - 1 : -1]
    for place in range(HEADS):
        h, weight = weight_rows(ids_ref, weight_refs, place)
        tile_ref[h] = dot(grad_ref[0], weight, NT).astype(BF16)
    for k, ref in enumerate(piece_refs):
        ref[...] = tile_ref[ids_ref[0] ^ k]


def output_body(ids_ref, back_ref, *refs):
    *weight_refs, out_ref = refs
    total = jnp.zeros(out_ref.shape[1:], F32)
    for place in range(HEADS):
        h, weight = weight_rows(ids_ref, weight_refs, place)
        total += dot(back_ref[h], weight, TN)
    out_ref[0] = total.astype(BF16)


def second_block(ids_ref, kb_ref, j, group):
    block = kb_ref[0, ids_ref[0], j * group + ids_ref[1], 1]
    return (block % group) ^ ids_ref[1], block // group


def forward_body(group, ids_ref, kb_ref, cnt_ref, *refs):
    own_ref, *other_refs = refs[:group]
    send_ref, probs_ref, kv_ref, s_ref, p_ref, t_ref, sems = refs[group:]
    kv_ref[0] = own_ref[:, BLOCK:, :]
    for r, ref in enumerate(other_refs):
        kv_ref[r + 1] = ref[:, BLOCK:, :]
    picks = [second_block(ids_ref, kb_ref, j, group) for j in range(HEADS)]
    copies = []
    for j in range(HEADS):
        q = own_ref[j, :BLOCK, :]
        both = cnt_ref[0, ids_ref[0], j * group + ids_ref[1]] > 1
        s_ref[j, :, :BLOCK] = dot(q, kv_ref[0, j, :BLOCK, :], NT) * SCALE
        s1 = dot(q, kv_ref[picks[j][0], picks[j][1], :BLOCK, :], NT) * SCALE
        s_ref[j, :, BLOCK:] = jnp.where(both, s1, -jnp.inf)
    for j in range(HEADS):
        s = s_ref[j]
        e = jnp.exp(s - jnp.max(s, axis=-1, keepdims=True))
        p = e * (1.0 / jnp.sum(e, axis=-1, keepdims=True))
        p_ref[j] = p.astype(BF16)
    copies.append(pltpu.make_async_copy(p_ref, probs_ref, sems.at[0]))
    copies[-1].start()
    for j in range(HEADS):
        attn = dot(p_ref[j, :, :BLOCK], kv_ref[0, j, BLOCK:, :], NN) + dot(
            p_ref[j, :, BLOCK:], kv_ref[picks[j][0], picks[j][1], BLOCK:, :], NN
        )
        t_ref[j] = attn.T.astype(BF16)
    copies.append(pltpu.make_async_copy(t_ref, send_ref, sems.at[1]))
    copies[-1].start()
    for copy in copies:
        copy.wait()


def backward_body(group, ids_ref, kb_ref, *refs):
    piece_refs, refs = refs[:HEADS], refs[HEADS:]
    own_ref, *other_refs = refs[:group]
    probs_ref, dq_ref, near_ref, *far_refs = refs[group:-8]
    q_ref, kv_ref, do_ref, p_ref, dp_ref, ds_ref, acc_ref, sems = refs[-8:]
    loads = [pltpu.make_async_copy(own_ref.at[:, pl.ds(BLOCK, 2 * BLOCK), :], kv_ref.at[0], sems.at[0])]
    for r, ref in enumerate(other_refs):
        loads.append(
            pltpu.make_async_copy(ref.at[:, pl.ds(BLOCK, 2 * BLOCK), :], kv_ref.at[r + 1], sems.at[r + 1])
        )
    loads.append(pltpu.make_async_copy(probs_ref, p_ref, sems.at[group]))
    loads.append(pltpu.make_async_copy(own_ref.at[:, pl.ds(0, BLOCK), :], q_ref, sems.at[group + 1]))
    for copy in loads:
        copy.start()
    for k, ref in enumerate(piece_refs):
        do_ref[ids_ref[0] ^ k] = ref[...]
    picks = [second_block(ids_ref, kb_ref, j, group) for j in range(HEADS)]
    for r in range(1, group):
        acc_ref[r] = jnp.zeros(acc_ref.shape[1:], F32)
    for copy in loads[:group]:
        copy.wait()
    for j in range(HEADS):
        do = do_ref[j]
        dp_ref[j, :, :BLOCK] = dot(do, kv_ref[0, j, BLOCK:, :], NT)
        dp_ref[j, :, BLOCK:] = dot(do, kv_ref[picks[j][0], picks[j][1], BLOCK:, :], NT)
    for copy in loads[group:]:
        copy.wait()
    for j in range(HEADS):
        p = p_ref[j].astype(F32)
        dp = dp_ref[j]
        delta = jnp.sum(p * dp, axis=-1, keepdims=True)
        ds_ref[j] = (p * (dp - delta)).astype(BF16)
    second = []
    for j in range(HEADS):
        dk = dot(ds_ref[j], q_ref[j], TN)
        dv = dot(p_ref[j], do_ref[j], TN)
        acc_ref[0, j, :BLOCK, :] = dk[:BLOCK]
        acc_ref[0, j, BLOCK:, :] = dv[:BLOCK]
        dp_ref[j, :, :BLOCK] = dk[BLOCK:]
        dp_ref[j, :, BLOCK:] = dv[BLOCK:]
    for j in range(HEADS):
        r, jb = picks[j]
        acc_ref[r, jb, :BLOCK, :] += dp_ref[j, :, :BLOCK]
        acc_ref[r, jb, BLOCK:, :] += dp_ref[j, :, BLOCK:]
    for j in range(HEADS):
        dq_ref[j] = (
            (
                dot(ds_ref[j, :, :BLOCK], kv_ref[0, j, :BLOCK, :], NN)
                + dot(ds_ref[j, :, BLOCK:], kv_ref[picks[j][0], picks[j][1], :BLOCK, :], NN)
            )
            * SCALE
        ).astype(BF16)
    for r, ref in enumerate((near_ref, *far_refs)):
        ref[:, :BLOCK, :] = (acc_ref[r, :, :BLOCK, :] * SCALE).astype(BF16)
        ref[:, BLOCK:, :] = acc_ref[r, :, BLOCK:, :].astype(BF16)


def combine_body(dq_ref, near_ref, *refs):
    *arrived_refs, send_ref = refs
    send_ref[:, :BLOCK, :] = dq_ref[...]
    total = near_ref[...].astype(F32)
    for ref in arrived_refs:
        total += ref[...].astype(F32)
    send_ref[:, BLOCK:, :] = total.astype(BF16)


def feature_body(ids_ref, mine_ref, pair_ref, *out_refs):
    d, z, y, c = ids_ref[2], ids_ref[3], ids_ref[4], ids_ref[5]
    for yr, ref in enumerate(out_refs):
        first = pl.multiple_of((yr ^ y) * 64 + c * 32, 32)
        for place in range(HEADS):
            h = ((place >> 2) ^ d) * 4 + ((place & 3) ^ z)
            rows = slice(place * 32, (place + 1) * 32)
            ref[rows, :BLOCK] = mine_ref[h, pl.ds(first, 32), :]
            ref[rows, BLOCK:] = pair_ref[h, pl.ds(first, 32), :]


def grad_weight_body(*refs):
    attn_refs, grad_refs = refs[:2], refs[2:6]
    keep_ref, send_ref, rows_ref, sems = refs[6:]
    loads = [
        pltpu.make_async_copy(ref.at[0], rows_ref.at[i], sems.at[i]) for i, ref in enumerate(grad_refs)
    ]
    for copy in loads:
        copy.start()
    for copy in loads:
        copy.wait()
    half = keep_ref.shape[0]
    for place, ref in ((1, send_ref), (0, keep_ref)):
        rows = slice(place * half, (place + 1) * half)
        total = jnp.zeros(ref.shape, F32)
        for i, attn_ref in enumerate(attn_refs):
            total += dot(attn_ref[rows, :BLOCK], rows_ref[i], NN)
            total += dot(attn_ref[rows, BLOCK:], rows_ref[i + 2], NN)
        ref[...] = total.astype(ref.dtype)


def ctx_swap(x, mask):
    n = lax.axis_size("ctx")
    return lax.ppermute(x, "ctx", [(i, i ^ mask) for i in range(n)])


def dp_swap(x):
    return lax.ppermute(x, "dp", [(0, 1), (1, 0)])


def together(*values):
    return lax.optimization_barrier(values)


def own_features(ids, back):
    return call(
        feature_body, [shape((HEADS * 32, 2 * BLOCK))] * 2, n_smem=1, n_vmem=2, name="features"
    )(ids, back, ctx_swap(back, 1))


def reduce_weight(features, rows):
    columns = rows[0].shape[-1]
    keep, send = call(
        grad_weight_body,
        [shape((4 * 32, columns), F32), shape((4 * 32, columns))],
        [pltpu.VMEM((4, BLOCK, columns), BF16), pltpu.SemaphoreType.DMA((4,))],
        n_vmem=2, n_hbm=4, vmem=16, flops=2**35, name="grad_weight",
    )(features[0], ctx_swap(features[1], 2), *rows)
    total = (keep + dp_swap(send).astype(F32)).reshape(4, 32, columns)
    parts = [ctx_swap(total[zr].astype(BF16), 4 * zr) for zr in range(1, 4)]
    return total[0] + sum(part.astype(F32) for part in parts)


D_OUT_FLOPS = 2**32


def local(queries, keys, values, out_weight, out_grad, key_blocks, block_counts):
    ctx_count = lax.axis_size("ctx")
    dp_count = lax.axis_size("dp")
    group = ctx_count // HEADS
    position = lax.axis_index("ctx")
    small = dp_count == 2 and ctx_count == 16
    rank = lax.axis_index("dp") if dp_count == 2 else 0
    ids = jnp.stack(
        [position // group, position % group, rank, position >> 2, position >> 1 & 1, position & 1,
         position & 1 if dp_count == 2 else 0]
    ).astype(jnp.int32)
    columns = out_grad.shape[-1]
    peers = [[j * group + m for j in range(HEADS)] for m in range(group)]

    def exchange(x):
        return lax.all_to_all(x, "ctx", 0, 0, tiled=True, axis_index_groups=peers)

    if dp_count == 2:
        near, rows = out_weight, out_weight.shape[0] // 2
        half = dp_swap(lax.dynamic_slice_in_dim(near, (position & 1) * rows, rows, 0))
    if small:
        cross = [ctx_swap(out_grad, 1)]
    if dp_count == 2:
        far = [half, ctx_swap(half, 1)]
    else:
        near, *far = jnp.split(
            lax.all_gather(out_weight, "dp", axis=0, tiled=True), (HEADS * 64, HEADS * 96)
        )

    own = exchange(pack(queries, keys, values))
    pair = shape((HEADS, 2 * BLOCK, HEAD_SIZE))
    tile = shape((HEADS, BLOCK, HEAD_SIZE))
    tile_scratch = pltpu.VMEM(tile.shape, BF16)
    score = (HEADS, BLOCK, 2 * BLOCK)
    pieces = call(
        d_out_body, [shape((BLOCK, HEAD_SIZE))] * HEADS, [tile_scratch],
        n_smem=1, n_vmem=4, flops=D_OUT_FLOPS, name="d_out",
    )(ids, out_grad, near, *far)
    pieces = [pieces[0]] + [ctx_swap(pieces[k], k * group) for k in range(1, HEADS)]
    if small:
        own, cross[0], *pieces = together(own, cross[0], *pieces)
    else:
        own, *pieces = together(own, *pieces)
    others = [ctx_swap(own, r) for r in range(1, group)]
    vmem = 16 if group == 2 else 40
    kv_scratch = pltpu.VMEM((group, HEADS, 2 * BLOCK, HEAD_SIZE), BF16)
    send, probs = call(
        functools.partial(forward_body, group),
        [tile, shape(score)],
        [kv_scratch, pltpu.VMEM(score, F32), pltpu.VMEM(score, BF16), tile_scratch, pltpu.SemaphoreType.DMA((2,))],
        n_smem=3, n_vmem=group, out_specs=[HBM] * 2, vmem=vmem, name="forward",
    )(ids, key_blocks, block_counts, own, *others)
    back = exchange(send)
    if small:
        same = [out_grad, ctx_swap(out_grad, 2)]
        cross.append(ctx_swap(same[1], 1))
        back, same[1], cross[1] = together(back, same[1], cross[1])
    dq, near_kv, *far_kv = call(
        functools.partial(backward_body, group),
        [tile, pair] + [pair] * (group - 1),
        [
            tile_scratch, kv_scratch, tile_scratch, pltpu.VMEM(score, BF16), pltpu.VMEM(score, F32),
            pltpu.VMEM(score, BF16),
            pltpu.VMEM((group, HEADS, 2 * BLOCK, HEAD_SIZE), F32), pltpu.SemaphoreType.DMA((group + 2,)),
        ],
        n_smem=2, n_vmem=HEADS, n_hbm=group + 1, vmem=vmem, name="backward",
    )(ids, key_blocks, *pieces, own, *others, probs)
    arrived = [ctx_swap(part, r + 1) for r, part in enumerate(far_kv)]
    if small:
        features = own_features(ids, back)
    grads = exchange(
        call(
            combine_body, shape((HEADS, 3 * BLOCK, HEAD_SIZE)), n_vmem=group + 1,
            vmem=vmem, flops=2**33, name="combine",
        )(dq, near_kv, *arrived)
    )
    tokens = shape((1, BLOCK, HEADS * HEAD_SIZE))
    grad_queries, grad_keys, grad_values = call(unpack_body, [tokens] * 3, n_vmem=1, name="unpack")(grads)
    if small:
        grad_weight = reduce_weight(features, same + cross)
    else:
        grad_weight = lax.psum_scatter(
            dot(back.reshape(HEADS * HEAD_SIZE, BLOCK), out_grad[0], NN),
            ("dp", "ctx"), scatter_dimension=0, tiled=True,
        )
    output = call(
        output_body, shape((1, BLOCK, columns)), n_smem=1, n_vmem=4, vmem=60, name="output",
    )(ids, back, near, *far)
    return (output, grad_queries, grad_keys, grad_values, grad_weight)


def solution(mesh):
    tokens = P("dp", "ctx", None)
    return jax.shard_map(
        local,
        mesh=mesh,
        in_specs=(
            tokens, tokens, tokens, P("dp", None), tokens,
            P("dp", None, None, None), P("dp", None, None),
        ),
        out_specs=(tokens, tokens, tokens, tokens, P(("dp", "ctx"), None)),
        check_vma=False,
    )
```

```python
import functools

import jax
import jax.numpy as jnp
from jax import lax
from jax.experimental import pallas as pl
from jax.experimental.pallas import tpu as pltpu
from jax.sharding import PartitionSpec as P

HEADS = 8
HEAD_SIZE = 128
BLOCK = 128
SCALE = HEAD_SIZE ** (-0.5)
F32 = jnp.float32
BF16 = jnp.bfloat16
VMEM = pl.BlockSpec(memory_space=pltpu.VMEM)
HBM = pl.BlockSpec(memory_space=pltpu.HBM)
SMEM = pl.BlockSpec(memory_space=pltpu.SMEM)
NN = (((1,), (0,)), ((), ()))
NT = (((1,), (1,)), ((), ()))
TN = (((0,), (0,)), ((), ()))


def dot(a, b, dims):
    return lax.dot_general(a, b, dims, preferred_element_type=F32)


def call(body, outs, scratch=(), n_smem=0, n_vmem=0, n_hbm=0, out_specs=None, vmem=16, alias=None, flops=0, name=None):
    many = isinstance(outs, (list, tuple))
    return pl.pallas_call(
        body,
        out_shape=outs,
        in_specs=[SMEM] * n_smem + [VMEM] * n_vmem + [HBM] * n_hbm,
        out_specs=out_specs or ([VMEM] * len(outs) if many else VMEM),
        scratch_shapes=list(scratch),
        input_output_aliases=alias or {},
        compiler_params=pltpu.CompilerParams(vmem_limit_bytes=vmem * 2**20),
        cost_estimate=pl.CostEstimate(flops=flops, bytes_accessed=0, transcendentals=0),
        name=name,
    )


def shape(dims, dtype=BF16):
    return jax.ShapeDtypeStruct(dims, dtype)


def head_lanes(h):
    return slice(h * HEAD_SIZE, (h + 1) * HEAD_SIZE)


def pack_body(q_ref, k_ref, v_ref, send_ref, wide_ref, tall_ref, in_sems, out_sems):
    inward = [
        pltpu.make_async_copy(ref.at[0], wide_ref.at[part], in_sems.at[part])
        for part, ref in enumerate((q_ref, k_ref, v_ref))
    ]
    outward = [
        pltpu.make_async_copy(
            tall_ref.at[part], send_ref.at[:, pl.ds(part * BLOCK, BLOCK), :], out_sems.at[part]
        )
        for part in range(3)
    ]
    for copy in inward:
        copy.start()
    for part in range(3):
        inward[part].wait()
        for h in range(HEADS):
            tall_ref[part, h] = wide_ref[part, :, head_lanes(h)]
        outward[part].start()
    for copy in outward:
        copy.wait()


def pack(*arrays):
    width = arrays[0].shape[-1]
    return pl.pallas_call(
        pack_body,
        out_shape=shape((HEADS, 3 * BLOCK, HEAD_SIZE)),
        in_specs=[HBM] * 3,
        out_specs=HBM,
        scratch_shapes=[
            pltpu.VMEM((3, BLOCK, width), BF16),
            pltpu.VMEM((3, HEADS, BLOCK, HEAD_SIZE), BF16),
            pltpu.SemaphoreType.DMA((3,)),
            pltpu.SemaphoreType.DMA((3,)),
        ],
        compiler_params=pltpu.CompilerParams(vmem_limit_bytes=60 * 2**20),
        cost_estimate=pl.CostEstimate(flops=2**35, bytes_accessed=0, transcendentals=0),
        name="pack",
    )(*arrays)


def unpack_body(recv_ref, q_ref, k_ref, v_ref):
    for part, ref in enumerate((q_ref, k_ref, v_ref)):
        for h in range(HEADS):
            ref[0, :, head_lanes(h)] = recv_ref[h, part * BLOCK : (part + 1) * BLOCK, :]


def weight_rows(ids_ref, refs, place):
    half, quarter = HEADS // 2, HEADS // 4
    i = place % quarter
    near_ref, *far_refs = refs
    if place < half:
        return ids_ref[2] * half + place, near_ref[place * HEAD_SIZE : (place + 1) * HEAD_SIZE, :]
    part = (place - half) // quarter
    h = (ids_ref[2] ^ 1) * half + (part ^ ids_ref[6]) * quarter + i
    return h, far_refs[part][i * HEAD_SIZE : (i + 1) * HEAD_SIZE, :]


def d_out_body(ids_ref, grad_ref, *refs):
    *weight_refs, tile_ref = refs[: -HEADS - 1] + refs[-1:]
    piece_refs = refs[-HEADS - 1 : -1]
    for place in range(HEADS):
        h, weight = weight_rows(ids_ref, weight_refs, place)
        tile_ref[h] = dot(grad_ref[0], weight, NT).astype(BF16)
    for k, ref in enumerate(piece_refs):
        ref[...] = tile_ref[ids_ref[0] ^ k]


def output_body(ids_ref, back_ref, *refs):
    *weight_refs, out_ref = refs
    total = jnp.zeros(out_ref.shape[1:], F32)
    for place in range(HEADS):
        h, weight = weight_rows(ids_ref, weight_refs, place)
        total += dot(back_ref[h], weight, TN)
    out_ref[0] = total.astype(BF16)


def second_block(ids_ref, kb_ref, j, group):
    block = kb_ref[0, ids_ref[0], j * group + ids_ref[1], 1]
    return (block % group) ^ ids_ref[1], block // group


def forward_body(group, ids_ref, kb_ref, cnt_ref, *refs):
    own_ref, *other_refs = refs[:group]
    send_ref, probs_ref, kv_ref, s_ref, p_ref, t_ref, sems = refs[group:]
    kv_ref[0] = own_ref[:, BLOCK:, :]
    for r, ref in enumerate(other_refs):
        kv_ref[r + 1] = ref[:, BLOCK:, :]
    picks = [second_block(ids_ref, kb_ref, j, group) for j in range(HEADS)]
    copies = []
    for j in range(HEADS):
        q = own_ref[j, :BLOCK, :]
        both = cnt_ref[0, ids_ref[0], j * group + ids_ref[1]] > 1
        s_ref[j, :, :BLOCK] = dot(q, kv_ref[0, j, :BLOCK, :], NT) * SCALE
        s1 = dot(q, kv_ref[picks[j][0], picks[j][1], :BLOCK, :], NT) * SCALE
        s_ref[j, :, BLOCK:] = jnp.where(both, s1, -jnp.inf)
    for j in range(HEADS):
        s = s_ref[j]
        e = jnp.exp(s - jnp.max(s, axis=-1, keepdims=True))
        p = e * (1.0 / jnp.sum(e, axis=-1, keepdims=True))
        p_ref[j] = p.astype(BF16)
    copies.append(pltpu.make_async_copy(p_ref, probs_ref, sems.at[0]))
    copies[-1].start()
    for j in range(HEADS):
        attn = dot(p_ref[j, :, :BLOCK], kv_ref[0, j, BLOCK:, :], NN) + dot(
            p_ref[j, :, BLOCK:], kv_ref[picks[j][0], picks[j][1], BLOCK:, :], NN
        )
        t_ref[j] = attn.T.astype(BF16)
    copies.append(pltpu.make_async_copy(t_ref, send_ref, sems.at[1]))
    copies[-1].start()
    for copy in copies:
        copy.wait()


def backward_body(group, ids_ref, kb_ref, *refs):
    piece_refs, refs = refs[:HEADS], refs[HEADS:]
    own_ref, *other_refs = refs[:group]
    probs_ref, dq_ref, near_ref, *far_refs = refs[group:-8]
    q_ref, kv_ref, do_ref, p_ref, dp_ref, ds_ref, acc_ref, sems = refs[-8:]
    loads = [pltpu.make_async_copy(own_ref.at[:, pl.ds(BLOCK, 2 * BLOCK), :], kv_ref.at[0], sems.at[0])]
    for r, ref in enumerate(other_refs):
        loads.append(
            pltpu.make_async_copy(ref.at[:, pl.ds(BLOCK, 2 * BLOCK), :], kv_ref.at[r + 1], sems.at[r + 1])
        )
    loads.append(pltpu.make_async_copy(probs_ref, p_ref, sems.at[group]))
    loads.append(pltpu.make_async_copy(own_ref.at[:, pl.ds(0, BLOCK), :], q_ref, sems.at[group + 1]))
    for copy in loads:
        copy.start()
    for k, ref in enumerate(piece_refs):
        do_ref[ids_ref[0] ^ k] = ref[...]
    picks = [second_block(ids_ref, kb_ref, j, group) for j in range(HEADS)]
    for r in range(1, group):
        acc_ref[r] = jnp.zeros(acc_ref.shape[1:], F32)
    for copy in loads[:group]:
        copy.wait()
    for j in range(HEADS):
        do = do_ref[j]
        dp_ref[j, :, :BLOCK] = dot(do, kv_ref[0, j, BLOCK:, :], NT)
        dp_ref[j, :, BLOCK:] = dot(do, kv_ref[picks[j][0], picks[j][1], BLOCK:, :], NT)
    for copy in loads[group:]:
        copy.wait()
    for j in range(HEADS):
        p = p_ref[j].astype(F32)
        dp = dp_ref[j]
        delta = jnp.sum(p * dp, axis=-1, keepdims=True)
        ds_ref[j] = (p * (dp - delta)).astype(BF16)
    second = []
    for j in range(HEADS):
        dk = dot(ds_ref[j], q_ref[j], TN)
        dv = dot(p_ref[j], do_ref[j], TN)
        acc_ref[0, j, :BLOCK, :] = dk[:BLOCK]
        acc_ref[0, j, BLOCK:, :] = dv[:BLOCK]
        dp_ref[j, :, :BLOCK] = dk[BLOCK:]
        dp_ref[j, :, BLOCK:] = dv[BLOCK:]
    for j in range(HEADS):
        r, jb = picks[j]
        acc_ref[r, jb, :BLOCK, :] += dp_ref[j, :, :BLOCK]
        acc_ref[r, jb, BLOCK:, :] += dp_ref[j, :, BLOCK:]
    for j in range(HEADS):
        dq_ref[j] = (
            (
                dot(ds_ref[j, :, :BLOCK], kv_ref[0, j, :BLOCK, :], NN)
                + dot(ds_ref[j, :, BLOCK:], kv_ref[picks[j][0], picks[j][1], :BLOCK, :], NN)
            )
            * SCALE
        ).astype(BF16)
    near_ref[:, :BLOCK, :] = (acc_ref[0, :, :BLOCK, :] * SCALE).astype(BF16)
    near_ref[:, BLOCK:, :] = acc_ref[0, :, BLOCK:, :].astype(BF16)
    for r in range(1, group):
        far_refs[2 * r - 2][...] = (acc_ref[r, :, :BLOCK, :] * SCALE).astype(BF16)
        far_refs[2 * r - 1][...] = acc_ref[r, :, BLOCK:, :].astype(BF16)


def combine_body(dq_ref, near_ref, *refs):
    *arrived_refs, send_ref = refs
    send_ref[:, :BLOCK, :] = dq_ref[...]
    for part in range(2):
        rows = slice(part * BLOCK, (part + 1) * BLOCK)
        total = near_ref[:, rows, :].astype(F32)
        for ref in arrived_refs[part::2]:
            total += ref[...].astype(F32)
        send_ref[:, BLOCK + part * BLOCK : 2 * BLOCK + part * BLOCK, :] = total.astype(BF16)


def feature_body(ids_ref, mine_ref, pair_ref, *out_refs):
    d, z, y, c = ids_ref[2], ids_ref[3], ids_ref[4], ids_ref[5]
    for yr, ref in enumerate(out_refs):
        first = pl.multiple_of((yr ^ y) * 64 + c * 32, 32)
        for place in range(HEADS):
            h = ((place >> 2) ^ d) * 4 + ((place & 3) ^ z)
            rows = slice(place * 32, (place + 1) * 32)
            ref[rows, :BLOCK] = mine_ref[h, pl.ds(first, 32), :]
            ref[rows, BLOCK:] = pair_ref[h, pl.ds(first, 32), :]


def grad_weight_body(*refs):
    attn_refs, grad_refs = refs[:2], refs[2:6]
    keep_ref, send_ref, rows_ref, sems = refs[6:]
    loads = [
        pltpu.make_async_copy(ref.at[0], rows_ref.at[i], sems.at[i]) for i, ref in enumerate(grad_refs)
    ]
    for copy in loads:
        copy.start()
    for copy in loads:
        copy.wait()
    half = keep_ref.shape[0]
    for place, ref in ((1, send_ref), (0, keep_ref)):
        rows = slice(place * half, (place + 1) * half)
        total = jnp.zeros(ref.shape, F32)
        for i, attn_ref in enumerate(attn_refs):
            total += dot(attn_ref[rows, :BLOCK], rows_ref[i], NN)
            total += dot(attn_ref[rows, BLOCK:], rows_ref[i + 2], NN)
        ref[...] = total.astype(ref.dtype)


def ctx_swap(x, mask):
    n = lax.axis_size("ctx")
    return lax.ppermute(x, "ctx", [(i, i ^ mask) for i in range(n)])


def dp_swap(x):
    return lax.ppermute(x, "dp", [(0, 1), (1, 0)])


def together(*values):
    return lax.optimization_barrier(values)


def own_features(ids, back):
    return call(
        feature_body, [shape((HEADS * 32, 2 * BLOCK))] * 2, n_smem=1, n_vmem=2, name="features"
    )(ids, back, ctx_swap(back, 1))


def reduce_weight(features, rows):
    columns = rows[0].shape[-1]
    keep, send = call(
        grad_weight_body,
        [shape((4 * 32, columns), F32), shape((4 * 32, columns))],
        [pltpu.VMEM((4, BLOCK, columns), BF16), pltpu.SemaphoreType.DMA((4,))],
        n_vmem=2, n_hbm=4, vmem=16, flops=GW_FLOPS, name="grad_weight",
    )(features[0], ctx_swap(features[1], 2), *rows)
    total = (keep + dp_swap(send).astype(F32)).reshape(4, 32, columns)
    parts = [ctx_swap(total[zr].astype(BF16), 4 * zr) for zr in range(1, 4)]
    return total[0] + sum(part.astype(F32) for part in parts)


D_OUT_FLOPS = 2**32
GW_FLOPS = 2**35


def local(queries, keys, values, out_weight, out_grad, key_blocks, block_counts):
    ctx_count = lax.axis_size("ctx")
    dp_count = lax.axis_size("dp")
    group = ctx_count // HEADS
    position = lax.axis_index("ctx")
    small = dp_count == 2 and ctx_count == 16
    rank = lax.axis_index("dp") if dp_count == 2 else 0
    ids = jnp.stack(
        [position // group, position % group, rank, position >> 2, position >> 1 & 1, position & 1,
         position & 1 if dp_count == 2 else 0]
    ).astype(jnp.int32)
    columns = out_grad.shape[-1]
    peers = [[j * group + m for j in range(HEADS)] for m in range(group)]

    def exchange(x):
        return lax.all_to_all(x, "ctx", 0, 0, tiled=True, axis_index_groups=peers)

    if dp_count == 2:
        near, rows = out_weight, out_weight.shape[0] // 2
        half = dp_swap(lax.dynamic_slice_in_dim(near, (position & 1) * rows, rows, 0))
    if small:
        cross = [ctx_swap(out_grad, 1)]
    if dp_count == 2:
        far = [half, ctx_swap(half, 1)]
    else:
        near, *far = jnp.split(
            lax.all_gather(out_weight, "dp", axis=0, tiled=True), (HEADS * 64, HEADS * 96)
        )

    own = exchange(pack(queries, keys, values))
    pair = shape((HEADS, 2 * BLOCK, HEAD_SIZE))
    tile = shape((HEADS, BLOCK, HEAD_SIZE))
    tile_scratch = pltpu.VMEM(tile.shape, BF16)
    score = (HEADS, BLOCK, 2 * BLOCK)
    pieces = call(
        d_out_body, [shape((BLOCK, HEAD_SIZE))] * HEADS, [tile_scratch],
        n_smem=1, n_vmem=4, flops=D_OUT_FLOPS, name="d_out",
    )(ids, out_grad, near, *far)
    pieces = [pieces[0]] + [ctx_swap(pieces[k], k * group) for k in range(1, HEADS)]
    if small:
        own, cross[0], *pieces = together(own, cross[0], *pieces)
    else:
        own, *pieces = together(own, *pieces)
    others = [ctx_swap(own, r) for r in range(1, group)]
    vmem = 16 if group == 2 else 40
    kv_scratch = pltpu.VMEM((group, HEADS, 2 * BLOCK, HEAD_SIZE), BF16)
    send, probs = call(
        functools.partial(forward_body, group),
        [tile, shape(score)],
        [kv_scratch, pltpu.VMEM(score, F32), pltpu.VMEM(score, BF16), tile_scratch, pltpu.SemaphoreType.DMA((2,))],
        n_smem=3, n_vmem=group, out_specs=[HBM] * 2, vmem=vmem, name="forward",
    )(ids, key_blocks, block_counts, own, *others)
    back = exchange(send)
    if small:
        same = [out_grad, ctx_swap(out_grad, 2)]
        cross.append(ctx_swap(same[1], 1))
        back, same[1], cross[1] = together(back, same[1], cross[1])
    dq, near_kv, *far_kv = call(
        functools.partial(backward_body, group),
        [tile, pair] + [tile] * (2 * group - 2),
        [
            tile_scratch, kv_scratch, tile_scratch, pltpu.VMEM(score, BF16), pltpu.VMEM(score, F32),
            pltpu.VMEM(score, BF16),
            pltpu.VMEM((group, HEADS, 2 * BLOCK, HEAD_SIZE), F32), pltpu.SemaphoreType.DMA((group + 2,)),
        ],
        n_smem=2, n_vmem=HEADS, n_hbm=group + 1, vmem=vmem, name="backward",
    )(ids, key_blocks, *pieces, own, *others, probs)
    arrived = [ctx_swap(part, i // 2 + 1) for i, part in enumerate(far_kv)]
    send = call(
        combine_body, shape((HEADS, 3 * BLOCK, HEAD_SIZE)), n_vmem=2 * group, vmem=vmem,
        name="combine",
    )(dq, near_kv, *arrived)
    back, send = together(back, send)
    grads = exchange(send)
    tokens = shape((1, BLOCK, HEADS * HEAD_SIZE))
    grad_queries, grad_keys, grad_values = call(unpack_body, [tokens] * 3, n_vmem=1, name="unpack")(grads)
    if small:
        grad_weight = reduce_weight(own_features(ids, back), same + cross)
    else:
        grad_weight = lax.psum_scatter(
            dot(back.reshape(HEADS * HEAD_SIZE, BLOCK), out_grad[0], NN),
            ("dp", "ctx"), scatter_dimension=0, tiled=True,
        )
    output = call(
        output_body, shape((1, BLOCK, columns)), n_smem=1, n_vmem=4, vmem=60, name="output",
    )(ids, back, near, *far)
    return (output, grad_queries, grad_keys, grad_values, grad_weight)


def solution(mesh):
    tokens = P("dp", "ctx", None)
    return jax.shard_map(
        local,
        mesh=mesh,
        in_specs=(
            tokens, tokens, tokens, P("dp", None), tokens,
            P("dp", None, None, None), P("dp", None, None),
        ),
        out_specs=(tokens, tokens, tokens, tokens, P(("dp", "ctx"), None)),
        check_vma=False,
    )
```

```python
import functools

import jax
import jax.numpy as jnp
from jax import lax
from jax.experimental import pallas as pl
from jax.experimental.pallas import tpu as pltpu
from jax.sharding import PartitionSpec as P

HEADS = 8
HEAD_SIZE = 128
BLOCK = 128
SCALE = HEAD_SIZE ** (-0.5)
F32 = jnp.float32
BF16 = jnp.bfloat16
VMEM = pl.BlockSpec(memory_space=pltpu.VMEM)
HBM = pl.BlockSpec(memory_space=pltpu.HBM)
SMEM = pl.BlockSpec(memory_space=pltpu.SMEM)
NN = (((1,), (0,)), ((), ()))
NT = (((1,), (1,)), ((), ()))
TN = (((0,), (0,)), ((), ()))


def dot(a, b, dims):
    return lax.dot_general(a, b, dims, preferred_element_type=F32)


def call(body, outs, scratch=(), n_smem=0, n_vmem=0, n_hbm=0, out_specs=None, vmem=16, alias=None, flops=0, name=None):
    many = isinstance(outs, (list, tuple))
    return pl.pallas_call(
        body,
        out_shape=outs,
        in_specs=[SMEM] * n_smem + [VMEM] * n_vmem + [HBM] * n_hbm,
        out_specs=out_specs or ([VMEM] * len(outs) if many else VMEM),
        scratch_shapes=list(scratch),
        input_output_aliases=alias or {},
        compiler_params=pltpu.CompilerParams(vmem_limit_bytes=vmem * 2**20),
        cost_estimate=pl.CostEstimate(flops=flops, bytes_accessed=0, transcendentals=0),
        name=name,
    )


def shape(dims, dtype=BF16):
    return jax.ShapeDtypeStruct(dims, dtype)


def head_lanes(h):
    return slice(h * HEAD_SIZE, (h + 1) * HEAD_SIZE)


def pack_body(q_ref, k_ref, v_ref, send_ref, wide_ref, tall_ref, in_sems, out_sems):
    inward = [
        pltpu.make_async_copy(ref.at[0], wide_ref.at[part], in_sems.at[part])
        for part, ref in enumerate((q_ref, k_ref, v_ref))
    ]
    outward = [
        pltpu.make_async_copy(
            tall_ref.at[part], send_ref.at[:, pl.ds(part * BLOCK, BLOCK), :], out_sems.at[part]
        )
        for part in range(3)
    ]
    for copy in inward:
        copy.start()
    for part in range(3):
        inward[part].wait()
        for h in range(HEADS):
            tall_ref[part, h] = wide_ref[part, :, head_lanes(h)]
        outward[part].start()
    for copy in outward:
        copy.wait()


def pack(*arrays):
    width = arrays[0].shape[-1]
    return pl.pallas_call(
        pack_body,
        out_shape=shape((HEADS, 3 * BLOCK, HEAD_SIZE)),
        in_specs=[HBM] * 3,
        out_specs=HBM,
        scratch_shapes=[
            pltpu.VMEM((3, BLOCK, width), BF16),
            pltpu.VMEM((3, HEADS, BLOCK, HEAD_SIZE), BF16),
            pltpu.SemaphoreType.DMA((3,)),
            pltpu.SemaphoreType.DMA((3,)),
        ],
        compiler_params=pltpu.CompilerParams(vmem_limit_bytes=60 * 2**20),
        cost_estimate=pl.CostEstimate(flops=2**35, bytes_accessed=0, transcendentals=0),
        name="pack",
    )(*arrays)


def unpack_body(recv_ref, q_ref, k_ref, v_ref):
    for part, ref in enumerate((q_ref, k_ref, v_ref)):
        for h in range(HEADS):
            ref[0, :, head_lanes(h)] = recv_ref[h, part * BLOCK : (part + 1) * BLOCK, :]


def weight_rows(ids_ref, refs, place):
    half, quarter = HEADS // 2, HEADS // 4
    i = place % quarter
    near_ref, *far_refs = refs
    if place < half:
        return ids_ref[2] * half + place, near_ref[place * HEAD_SIZE : (place + 1) * HEAD_SIZE, :]
    part = (place - half) // quarter
    h = (ids_ref[2] ^ 1) * half + (part ^ ids_ref[6]) * quarter + i
    return h, far_refs[part][i * HEAD_SIZE : (i + 1) * HEAD_SIZE, :]


def d_out_body(ids_ref, grad_ref, *refs):
    *weight_refs, tile_ref = refs[: -HEADS - 1] + refs[-1:]
    piece_refs = refs[-HEADS - 1 : -1]
    for place in range(HEADS):
        h, weight = weight_rows(ids_ref, weight_refs, place)
        tile_ref[h] = dot(grad_ref[0], weight, NT).astype(BF16)
    for k, ref in enumerate(piece_refs):
        ref[...] = tile_ref[ids_ref[0] ^ k]


def output_body(ids_ref, back_ref, *refs):
    *weight_refs, out_ref = refs
    total = jnp.zeros(out_ref.shape[1:], F32)
    for place in range(HEADS):
        h, weight = weight_rows(ids_ref, weight_refs, place)
        total += dot(back_ref[h], weight, TN)
    out_ref[0] = total.astype(BF16)


def second_block(ids_ref, kb_ref, j, group):
    block = kb_ref[0, ids_ref[0], j * group + ids_ref[1], 1]
    return (block % group) ^ ids_ref[1], block // group


KEYS, VALUES = slice(0, BLOCK), slice(BLOCK, 2 * BLOCK)


def both_blocks(kv_ref, j, picks, rows):
    return jnp.concatenate([kv_ref[0, j, rows, :], kv_ref[picks[j][0], picks[j][1], rows, :]], axis=0)


def forward_body(group, ids_ref, kb_ref, cnt_ref, *refs):
    own_ref, *other_refs = refs[:group]
    send_ref, probs_ref, kv_ref, s_ref, p_ref, t_ref, sems = refs[group:]
    kv_ref[0] = own_ref[:, BLOCK:, :]
    for r, ref in enumerate(other_refs):
        kv_ref[r + 1] = ref[:, BLOCK:, :]
    picks = [second_block(ids_ref, kb_ref, j, group) for j in range(HEADS)]
    copies = []
    for j in range(HEADS):
        q = own_ref[j, :BLOCK, :]
        both = cnt_ref[0, ids_ref[0], j * group + ids_ref[1]] > 1
        s = dot(q, both_blocks(kv_ref, j, picks, KEYS), NT) * SCALE
        s_ref[j, :, :BLOCK] = s[:, :BLOCK]
        s_ref[j, :, BLOCK:] = jnp.where(both, s[:, BLOCK:], -jnp.inf)
    for j in range(HEADS):
        s = s_ref[j]
        e = jnp.exp(s - jnp.max(s, axis=-1, keepdims=True))
        p = e * (1.0 / jnp.sum(e, axis=-1, keepdims=True))
        p_ref[j] = p.astype(BF16)
    copies.append(pltpu.make_async_copy(p_ref, probs_ref, sems.at[0]))
    copies[-1].start()
    for j in range(HEADS):
        attn = dot(p_ref[j], both_blocks(kv_ref, j, picks, VALUES), NN)
        t_ref[j] = attn.T.astype(BF16)
    copies.append(pltpu.make_async_copy(t_ref, send_ref, sems.at[1]))
    copies[-1].start()
    for copy in copies:
        copy.wait()


def backward_body(group, ids_ref, kb_ref, *refs):
    piece_refs, refs = refs[:HEADS], refs[HEADS:]
    own_ref, *other_refs = refs[:group]
    probs_ref, dq_ref, near_ref, *far_refs = refs[group:-8]
    q_ref, kv_ref, do_ref, p_ref, dp_ref, ds_ref, acc_ref, sems = refs[-8:]
    loads = [pltpu.make_async_copy(own_ref.at[:, pl.ds(BLOCK, 2 * BLOCK), :], kv_ref.at[0], sems.at[0])]
    for r, ref in enumerate(other_refs):
        loads.append(
            pltpu.make_async_copy(ref.at[:, pl.ds(BLOCK, 2 * BLOCK), :], kv_ref.at[r + 1], sems.at[r + 1])
        )
    loads.append(pltpu.make_async_copy(probs_ref, p_ref, sems.at[group]))
    loads.append(pltpu.make_async_copy(own_ref.at[:, pl.ds(0, BLOCK), :], q_ref, sems.at[group + 1]))
    for copy in loads:
        copy.start()
    for k, ref in enumerate(piece_refs):
        do_ref[ids_ref[0] ^ k] = ref[...]
    picks = [second_block(ids_ref, kb_ref, j, group) for j in range(HEADS)]
    for r in range(1, group):
        acc_ref[r] = jnp.zeros(acc_ref.shape[1:], F32)
    for copy in loads[:group]:
        copy.wait()
    for j in range(HEADS):
        do = do_ref[j]
        dp_ref[j] = dot(do, both_blocks(kv_ref, j, picks, VALUES), NT)
    for copy in loads[group:]:
        copy.wait()
    for j in range(HEADS):
        p = p_ref[j].astype(F32)
        dp = dp_ref[j]
        delta = jnp.sum(p * dp, axis=-1, keepdims=True)
        ds_ref[j] = (p * (dp - delta)).astype(BF16)
    second = []
    for j in range(HEADS):
        dk = dot(ds_ref[j], q_ref[j], TN)
        dv = dot(p_ref[j], do_ref[j], TN)
        acc_ref[0, j, :BLOCK, :] = dk[:BLOCK]
        acc_ref[0, j, BLOCK:, :] = dv[:BLOCK]
        dp_ref[j, :, :BLOCK] = dk[BLOCK:]
        dp_ref[j, :, BLOCK:] = dv[BLOCK:]
    for j in range(HEADS):
        r, jb = picks[j]
        acc_ref[r, jb, :BLOCK, :] += dp_ref[j, :, :BLOCK]
        acc_ref[r, jb, BLOCK:, :] += dp_ref[j, :, BLOCK:]
    for j in range(HEADS):
        dq_ref[j] = (dot(ds_ref[j], both_blocks(kv_ref, j, picks, KEYS), NN) * SCALE).astype(BF16)
    near_ref[:, :BLOCK, :] = (acc_ref[0, :, :BLOCK, :] * SCALE).astype(BF16)
    near_ref[:, BLOCK:, :] = acc_ref[0, :, BLOCK:, :].astype(BF16)
    for r in range(1, group):
        far_refs[2 * r - 2][...] = (acc_ref[r, :, :BLOCK, :] * SCALE).astype(BF16)
        far_refs[2 * r - 1][...] = acc_ref[r, :, BLOCK:, :].astype(BF16)


def combine_body(dq_ref, near_ref, *refs):
    *arrived_refs, send_ref = refs
    send_ref[:, :BLOCK, :] = dq_ref[...]
    for part in range(2):
        rows = slice(part * BLOCK, (part + 1) * BLOCK)
        total = near_ref[:, rows, :].astype(F32)
        for ref in arrived_refs[part::2]:
            total += ref[...].astype(F32)
        send_ref[:, BLOCK + part * BLOCK : 2 * BLOCK + part * BLOCK, :] = total.astype(BF16)


def feature_body(ids_ref, mine_ref, pair_ref, *out_refs):
    d, z, y, c = ids_ref[2], ids_ref[3], ids_ref[4], ids_ref[5]
    for yr, ref in enumerate(out_refs):
        first = pl.multiple_of((yr ^ y) * 64 + c * 32, 32)
        for place in range(HEADS):
            h = ((place >> 2) ^ d) * 4 + ((place & 3) ^ z)
            rows = slice(place * 32, (place + 1) * 32)
            ref[rows, :BLOCK] = mine_ref[h, pl.ds(first, 32), :]
            ref[rows, BLOCK:] = pair_ref[h, pl.ds(first, 32), :]


def grad_weight_body(*refs):
    attn_refs, grad_refs = refs[:2], refs[2:6]
    keep_ref, send_ref, rows_ref, sems = refs[6:]
    loads = [
        pltpu.make_async_copy(ref.at[0], rows_ref.at[i], sems.at[i]) for i, ref in enumerate(grad_refs)
    ]
    for copy in loads:
        copy.start()
    for copy in loads:
        copy.wait()
    half = keep_ref.shape[0]
    for place, ref in ((1, send_ref), (0, keep_ref)):
        rows = slice(place * half, (place + 1) * half)
        total = jnp.zeros(ref.shape, F32)
        for i, attn_ref in enumerate(attn_refs):
            total += dot(attn_ref[rows, :BLOCK], rows_ref[i], NN)
            total += dot(attn_ref[rows, BLOCK:], rows_ref[i + 2], NN)
        ref[...] = total.astype(ref.dtype)


def ctx_swap(x, mask):
    n = lax.axis_size("ctx")
    return lax.ppermute(x, "ctx", [(i, i ^ mask) for i in range(n)])


def dp_swap(x):
    return lax.ppermute(x, "dp", [(0, 1), (1, 0)])


def together(*values):
    return lax.optimization_barrier(values)


def own_features(ids, back):
    return call(
        feature_body, [shape((HEADS * 32, 2 * BLOCK))] * 2, n_smem=1, n_vmem=2, name="features"
    )(ids, back, ctx_swap(back, 1))


def reduce_weight(features, rows):
    columns = rows[0].shape[-1]
    keep, send = call(
        grad_weight_body,
        [shape((4 * 32, columns), F32), shape((4 * 32, columns))],
        [pltpu.VMEM((4, BLOCK, columns), BF16), pltpu.SemaphoreType.DMA((4,))],
        n_vmem=2, n_hbm=4, vmem=16, flops=GW_FLOPS, name="grad_weight",
    )(features[0], ctx_swap(features[1], 2), *rows)
    total = (keep + dp_swap(send).astype(F32)).reshape(4, 32, columns)
    return total[0], [ctx_swap(total[zr].astype(BF16), 4 * zr) for zr in range(1, 4)]


D_OUT_FLOPS = 2**32
GW_FLOPS = 2**35


def local(queries, keys, values, out_weight, out_grad, key_blocks, block_counts):
    ctx_count = lax.axis_size("ctx")
    dp_count = lax.axis_size("dp")
    group = ctx_count // HEADS
    position = lax.axis_index("ctx")
    small = dp_count == 2 and ctx_count == 16
    rank = lax.axis_index("dp") if dp_count == 2 else 0
    ids = jnp.stack(
        [position // group, position % group, rank, position >> 2, position >> 1 & 1, position & 1,
         position & 1 if dp_count == 2 else 0]
    ).astype(jnp.int32)
    columns = out_grad.shape[-1]
    peers = [[j * group + m for j in range(HEADS)] for m in range(group)]

    def exchange(x):
        return lax.all_to_all(x, "ctx", 0, 0, tiled=True, axis_index_groups=peers)

    if dp_count == 2:
        near, rows = out_weight, out_weight.shape[0] // 2
        half = dp_swap(lax.dynamic_slice_in_dim(near, (position & 1) * rows, rows, 0))
    if small:
        cross = [ctx_swap(out_grad, 1)]
    if dp_count == 2:
        far = [half, ctx_swap(half, 1)]
    else:
        near, *far = jnp.split(
            lax.all_gather(out_weight, "dp", axis=0, tiled=True), (HEADS * 64, HEADS * 96)
        )

    own = exchange(pack(queries, keys, values))
    pair = shape((HEADS, 2 * BLOCK, HEAD_SIZE))
    tile = shape((HEADS, BLOCK, HEAD_SIZE))
    tile_scratch = pltpu.VMEM(tile.shape, BF16)
    score = (HEADS, BLOCK, 2 * BLOCK)
    pieces = call(
        d_out_body, [shape((BLOCK, HEAD_SIZE))] * HEADS, [tile_scratch],
        n_smem=1, n_vmem=4, flops=D_OUT_FLOPS, name="d_out",
    )(ids, out_grad, near, *far)
    pieces = [pieces[0]] + [ctx_swap(pieces[k], k * group) for k in range(1, HEADS)]
    if small:
        own, cross[0], *pieces = together(own, cross[0], *pieces)
    else:
        own, *pieces = together(own, *pieces)
    others = [ctx_swap(own, r) for r in range(1, group)]
    vmem = 16 if group == 2 else 40
    kv_scratch = pltpu.VMEM((group, HEADS, 2 * BLOCK, HEAD_SIZE), BF16)
    send, probs = call(
        functools.partial(forward_body, group),
        [tile, shape(score)],
        [kv_scratch, pltpu.VMEM(score, F32), pltpu.VMEM(score, BF16), tile_scratch, pltpu.SemaphoreType.DMA((2,))],
        n_smem=3, n_vmem=group, out_specs=[HBM] * 2, vmem=vmem, name="forward",
    )(ids, key_blocks, block_counts, own, *others)
    back = exchange(send)
    if small:
        same = [out_grad, ctx_swap(out_grad, 2)]
        cross.append(ctx_swap(same[1], 1))
        back, same[1], cross[1] = together(back, same[1], cross[1])
    dq, near_kv, *far_kv = call(
        functools.partial(backward_body, group),
        [tile, pair] + [tile] * (2 * group - 2),
        [
            tile_scratch, kv_scratch, tile_scratch, pltpu.VMEM(score, BF16), pltpu.VMEM(score, F32),
            pltpu.VMEM(score, BF16),
            pltpu.VMEM((group, HEADS, 2 * BLOCK, HEAD_SIZE), F32), pltpu.SemaphoreType.DMA((group + 2,)),
        ],
        n_smem=2, n_vmem=HEADS, n_hbm=group + 1, vmem=vmem, name="backward",
    )(ids, key_blocks, *pieces, own, *others, probs)
    arrived = [ctx_swap(part, i // 2 + 1) for i, part in enumerate(far_kv)]
    send = call(
        combine_body, shape((HEADS, 3 * BLOCK, HEAD_SIZE)), n_vmem=2 * group, vmem=vmem,
        name="combine",
    )(dq, near_kv, *arrived)
    back, send = together(back, send)
    grads = exchange(send)
    tokens = shape((1, BLOCK, HEADS * HEAD_SIZE))
    grad_queries, grad_keys, grad_values = call(unpack_body, [tokens] * 3, n_vmem=1, name="unpack")(grads)
    if small:
        mine, parts = reduce_weight(own_features(ids, back), same + cross)
        mine, grad_queries, grad_keys, grad_values = together(
            mine, grad_queries, grad_keys, grad_values
        )
        grad_weight = mine + sum(part.astype(F32) for part in parts)
    else:
        grad_weight = lax.psum_scatter(
            dot(back.reshape(HEADS * HEAD_SIZE, BLOCK), out_grad[0], NN),
            ("dp", "ctx"), scatter_dimension=0, tiled=True,
        )
    output = call(
        output_body, shape((1, BLOCK, columns)), n_smem=1, n_vmem=4, vmem=60, name="output",
    )(ids, back, near, *far)
    return (output, grad_queries, grad_keys, grad_values, grad_weight)


def solution(mesh):
    tokens = P("dp", "ctx", None)
    return jax.shard_map(
        local,
        mesh=mesh,
        in_specs=(
            tokens, tokens, tokens, P("dp", None), tokens,
            P("dp", None, None, None), P("dp", None, None),
        ),
        out_specs=(tokens, tokens, tokens, tokens, P(("dp", "ctx"), None)),
        check_vma=False,
    )
```

```python
import functools

import jax
import jax.numpy as jnp
from jax import lax
from jax.experimental import pallas as pl
from jax.experimental.pallas import tpu as pltpu
from jax.sharding import PartitionSpec as P

HEADS = 8
HEAD_SIZE = 128
BLOCK = 128
SCALE = HEAD_SIZE ** (-0.5)
F32 = jnp.float32
BF16 = jnp.bfloat16
VMEM = pl.BlockSpec(memory_space=pltpu.VMEM)
HBM = pl.BlockSpec(memory_space=pltpu.HBM)
SMEM = pl.BlockSpec(memory_space=pltpu.SMEM)
NN = (((1,), (0,)), ((), ()))
NT = (((1,), (1,)), ((), ()))
TN = (((0,), (0,)), ((), ()))


def dot(a, b, dims):
    return lax.dot_general(a, b, dims, preferred_element_type=F32)


def call(body, outs, scratch=(), n_smem=0, n_vmem=0, n_hbm=0, out_specs=None, vmem=16, alias=None, flops=0, name=None):
    many = isinstance(outs, (list, tuple))
    return pl.pallas_call(
        body,
        out_shape=outs,
        in_specs=[SMEM] * n_smem + [VMEM] * n_vmem + [HBM] * n_hbm,
        out_specs=out_specs or ([VMEM] * len(outs) if many else VMEM),
        scratch_shapes=list(scratch),
        input_output_aliases=alias or {},
        compiler_params=pltpu.CompilerParams(vmem_limit_bytes=vmem * 2**20),
        cost_estimate=pl.CostEstimate(flops=flops, bytes_accessed=0, transcendentals=0),
        name=name,
    )


def shape(dims, dtype=BF16):
    return jax.ShapeDtypeStruct(dims, dtype)


def head_lanes(h):
    return slice(h * HEAD_SIZE, (h + 1) * HEAD_SIZE)


def pack_body(q_ref, k_ref, v_ref, send_ref, wide_ref, tall_ref, in_sems, out_sems):
    inward = [
        pltpu.make_async_copy(ref.at[0], wide_ref.at[part], in_sems.at[part])
        for part, ref in enumerate((q_ref, k_ref, v_ref))
    ]
    outward = [
        pltpu.make_async_copy(
            tall_ref.at[part], send_ref.at[:, pl.ds(part * BLOCK, BLOCK), :], out_sems.at[part]
        )
        for part in range(3)
    ]
    for copy in inward:
        copy.start()
    for part in range(3):
        inward[part].wait()
        for h in range(HEADS):
            tall_ref[part, h] = wide_ref[part, :, head_lanes(h)]
        outward[part].start()
    for copy in outward:
        copy.wait()


def pack(*arrays):
    width = arrays[0].shape[-1]
    return pl.pallas_call(
        pack_body,
        out_shape=shape((HEADS, 3 * BLOCK, HEAD_SIZE)),
        in_specs=[HBM] * 3,
        out_specs=HBM,
        scratch_shapes=[
            pltpu.VMEM((3, BLOCK, width), BF16),
            pltpu.VMEM((3, HEADS, BLOCK, HEAD_SIZE), BF16),
            pltpu.SemaphoreType.DMA((3,)),
            pltpu.SemaphoreType.DMA((3,)),
        ],
        compiler_params=pltpu.CompilerParams(vmem_limit_bytes=60 * 2**20),
        cost_estimate=pl.CostEstimate(flops=2**35, bytes_accessed=0, transcendentals=0),
        name="pack",
    )(*arrays)


def unpack_body(recv_ref, q_ref, k_ref, v_ref):
    for part, ref in enumerate((q_ref, k_ref, v_ref)):
        for h in range(HEADS):
            ref[0, :, head_lanes(h)] = recv_ref[h, part * BLOCK : (part + 1) * BLOCK, :]


def weight_rows(ids_ref, refs, place):
    half, quarter = HEADS // 2, HEADS // 4
    i = place % quarter
    near_ref, *far_refs = refs
    if place < half:
        return ids_ref[2] * half + place, near_ref[place * HEAD_SIZE : (place + 1) * HEAD_SIZE, :]
    part = (place - half) // quarter
    h = (ids_ref[2] ^ 1) * half + (part ^ ids_ref[6]) * quarter + i
    return h, far_refs[part][i * HEAD_SIZE : (i + 1) * HEAD_SIZE, :]


def d_out_body(ids_ref, grad_ref, *refs):
    *weight_refs, tile_ref = refs[: -HEADS - 1] + refs[-1:]
    piece_refs = refs[-HEADS - 1 : -1]
    for place in range(HEADS):
        h, weight = weight_rows(ids_ref, weight_refs, place)
        tile_ref[h] = dot(grad_ref[0], weight, NT).astype(BF16)
    for k, ref in enumerate(piece_refs):
        ref[...] = tile_ref[ids_ref[0] ^ k]


def output_body(ids_ref, back_ref, *refs):
    *weight_refs, out_ref = refs
    total = jnp.zeros(out_ref.shape[1:], F32)
    for place in range(HEADS):
        h, weight = weight_rows(ids_ref, weight_refs, place)
        total += dot(back_ref[h], weight, TN)
    out_ref[0] = total.astype(BF16)


def second_block(ids_ref, kb_ref, j, group):
    block = kb_ref[0, ids_ref[0], j * group + ids_ref[1], 1]
    return (block % group) ^ ids_ref[1], block // group


KEYS, VALUES = slice(0, BLOCK), slice(BLOCK, 2 * BLOCK)


def both_blocks(kv_ref, j, picks, rows):
    return jnp.concatenate([kv_ref[0, j, rows, :], kv_ref[picks[j][0], picks[j][1], rows, :]], axis=0)


def forward_body(group, ids_ref, kb_ref, cnt_ref, *refs):
    own_ref, *other_refs = refs[:group]
    send_ref, probs_ref, kv_ref, s_ref, p_ref, t_ref, sems = refs[group:]
    kv_ref[0] = own_ref[:, BLOCK:, :]
    for r, ref in enumerate(other_refs):
        kv_ref[r + 1] = ref[:, BLOCK:, :]
    picks = [second_block(ids_ref, kb_ref, j, group) for j in range(HEADS)]
    copies = []
    for j in range(HEADS):
        q = own_ref[j, :BLOCK, :]
        both = cnt_ref[0, ids_ref[0], j * group + ids_ref[1]] > 1
        s = dot(q, both_blocks(kv_ref, j, picks, KEYS), NT) * SCALE
        s_ref[j, :, :BLOCK] = s[:, :BLOCK]
        s_ref[j, :, BLOCK:] = jnp.where(both, s[:, BLOCK:], -jnp.inf)
    for j in range(HEADS):
        s = s_ref[j]
        e = jnp.exp(s - jnp.max(s, axis=-1, keepdims=True))
        p = e * (1.0 / jnp.sum(e, axis=-1, keepdims=True))
        p_ref[j] = p.astype(BF16)
    copies.append(pltpu.make_async_copy(p_ref, probs_ref, sems.at[0]))
    copies[-1].start()
    for j in range(HEADS):
        attn = dot(p_ref[j], both_blocks(kv_ref, j, picks, VALUES), NN)
        t_ref[j] = attn.T.astype(BF16)
    copies.append(pltpu.make_async_copy(t_ref, send_ref, sems.at[1]))
    copies[-1].start()
    for copy in copies:
        copy.wait()


def backward_body(group, ids_ref, kb_ref, *refs):
    piece_refs, refs = refs[:HEADS], refs[HEADS:]
    own_ref, *other_refs = refs[:group]
    probs_ref, dq_ref, near_ref, *far_refs = refs[group:-8]
    q_ref, kv_ref, do_ref, p_ref, dp_ref, ds_ref, acc_ref, sems = refs[-8:]
    loads = [pltpu.make_async_copy(own_ref.at[:, pl.ds(BLOCK, 2 * BLOCK), :], kv_ref.at[0], sems.at[0])]
    for r, ref in enumerate(other_refs):
        loads.append(
            pltpu.make_async_copy(ref.at[:, pl.ds(BLOCK, 2 * BLOCK), :], kv_ref.at[r + 1], sems.at[r + 1])
        )
    loads.append(pltpu.make_async_copy(probs_ref, p_ref, sems.at[group]))
    loads.append(pltpu.make_async_copy(own_ref.at[:, pl.ds(0, BLOCK), :], q_ref, sems.at[group + 1]))
    for copy in loads:
        copy.start()
    for k, ref in enumerate(piece_refs):
        do_ref[ids_ref[0] ^ k] = ref[...]
    picks = [second_block(ids_ref, kb_ref, j, group) for j in range(HEADS)]
    for r in range(1, group):
        acc_ref[r] = jnp.zeros(acc_ref.shape[1:], F32)
    for copy in loads[:group]:
        copy.wait()
    for j in range(HEADS):
        do = do_ref[j]
        dp_ref[j] = dot(do, both_blocks(kv_ref, j, picks, VALUES), NT)
    for copy in loads[group:]:
        copy.wait()
    for j in range(HEADS):
        p = p_ref[j].astype(F32)
        dp = dp_ref[j]
        delta = jnp.sum(p * dp, axis=-1, keepdims=True)
        ds_ref[j] = (p * (dp - delta)).astype(BF16)
    second = []
    for j in range(HEADS):
        dk = dot(ds_ref[j], q_ref[j], TN)
        dv = dot(p_ref[j], do_ref[j], TN)
        acc_ref[0, j, :BLOCK, :] = dk[:BLOCK]
        acc_ref[0, j, BLOCK:, :] = dv[:BLOCK]
        dp_ref[j, :, :BLOCK] = dk[BLOCK:]
        dp_ref[j, :, BLOCK:] = dv[BLOCK:]
    for j in range(HEADS):
        r, jb = picks[j]
        acc_ref[r, jb, :BLOCK, :] += dp_ref[j, :, :BLOCK]
        acc_ref[r, jb, BLOCK:, :] += dp_ref[j, :, BLOCK:]
    for j in range(HEADS):
        dq_ref[j] = (dot(ds_ref[j], both_blocks(kv_ref, j, picks, KEYS), NN) * SCALE).astype(BF16)
    near_ref[:, :BLOCK, :] = (acc_ref[0, :, :BLOCK, :] * SCALE).astype(BF16)
    near_ref[:, BLOCK:, :] = acc_ref[0, :, BLOCK:, :].astype(BF16)
    for r in range(1, group):
        far_refs[2 * r - 2][...] = (acc_ref[r, :, :BLOCK, :] * SCALE).astype(BF16)
        far_refs[2 * r - 1][...] = acc_ref[r, :, BLOCK:, :].astype(BF16)


def combine_body(dq_ref, near_ref, *refs):
    *arrived_refs, send_ref = refs
    send_ref[:, :BLOCK, :] = dq_ref[...]
    for part in range(2):
        rows = slice(part * BLOCK, (part + 1) * BLOCK)
        total = near_ref[:, rows, :].astype(F32)
        for ref in arrived_refs[part::2]:
            total += ref[...].astype(F32)
        send_ref[:, BLOCK + part * BLOCK : 2 * BLOCK + part * BLOCK, :] = total.astype(BF16)


def feature_body(ids_ref, mine_ref, *out_refs):
    d, z, y, c = ids_ref[2], ids_ref[3], ids_ref[4], ids_ref[5]
    for to, ref in enumerate(out_refs):
        first = pl.multiple_of(((to >> 1) ^ y) * 64 + ((to & 1) ^ c) * 32, 32)
        for place in range(HEADS):
            h = ((place >> 2) ^ d) * 4 + ((place & 3) ^ z)
            ref[place * 32 : (place + 1) * 32, :] = mine_ref[h, pl.ds(first, 32), :]


def grad_weight_body(*refs):
    attn_refs, grad_refs = refs[:4], refs[4:8]
    keep_ref, send_ref, rows_ref, sems = refs[8:]
    loads = [
        pltpu.make_async_copy(ref.at[0], rows_ref.at[i], sems.at[i]) for i, ref in enumerate(grad_refs)
    ]
    for copy in loads:
        copy.start()
    for copy in loads:
        copy.wait()
    half = keep_ref.shape[0]
    for place, ref in ((1, send_ref), (0, keep_ref)):
        rows = slice(place * half, (place + 1) * half)
        total = jnp.zeros(ref.shape, F32)
        for i, attn_ref in enumerate(attn_refs):
            total += dot(attn_ref[rows, :], rows_ref[i], NN)
        ref[...] = total.astype(ref.dtype)


def ctx_swap(x, mask):
    n = lax.axis_size("ctx")
    return lax.ppermute(x, "ctx", [(i, i ^ mask) for i in range(n)])


def dp_swap(x):
    return lax.ppermute(x, "dp", [(0, 1), (1, 0)])


def together(*values):
    return lax.optimization_barrier(values)


def own_features(ids, back):
    return call(
        feature_body, [shape((HEADS * 32, BLOCK))] * 4, n_smem=1, n_vmem=1, name="features"
    )(ids, back)


def reduce_weight(features, rows):
    columns = rows[0].shape[-1]
    attn = [features[0]] + [ctx_swap(features[to], to) for to in (1, 2, 3)]
    keep, send = call(
        grad_weight_body,
        [shape((4 * 32, columns), F32), shape((4 * 32, columns))],
        [pltpu.VMEM((4, BLOCK, columns), BF16), pltpu.SemaphoreType.DMA((4,))],
        n_vmem=4, n_hbm=4, vmem=16, flops=GW_FLOPS, name="grad_weight",
    )(*attn, *rows)
    total = (keep + dp_swap(send).astype(F32)).reshape(4, 32, columns)
    return total[0], [ctx_swap(total[zr].astype(BF16), 4 * zr) for zr in range(1, 4)]


D_OUT_FLOPS = 2**32
GW_FLOPS = 2**35


def local(queries, keys, values, out_weight, out_grad, key_blocks, block_counts):
    ctx_count = lax.axis_size("ctx")
    dp_count = lax.axis_size("dp")
    group = ctx_count // HEADS
    position = lax.axis_index("ctx")
    small = dp_count == 2 and ctx_count == 16
    rank = lax.axis_index("dp") if dp_count == 2 else 0
    ids = jnp.stack(
        [position // group, position % group, rank, position >> 2, position >> 1 & 1, position & 1,
         position & 1 if dp_count == 2 else 0]
    ).astype(jnp.int32)
    columns = out_grad.shape[-1]
    peers = [[j * group + m for j in range(HEADS)] for m in range(group)]

    def exchange(x):
        return lax.all_to_all(x, "ctx", 0, 0, tiled=True, axis_index_groups=peers)

    if dp_count == 2:
        near, rows = out_weight, out_weight.shape[0] // 2
        half = dp_swap(lax.dynamic_slice_in_dim(near, (position & 1) * rows, rows, 0))
    if small:
        cross = [ctx_swap(out_grad, 1)]
    if dp_count == 2:
        far = [half, ctx_swap(half, 1)]
    else:
        near, *far = jnp.split(
            lax.all_gather(out_weight, "dp", axis=0, tiled=True), (HEADS * 64, HEADS * 96)
        )

    own = exchange(pack(queries, keys, values))
    pair = shape((HEADS, 2 * BLOCK, HEAD_SIZE))
    tile = shape((HEADS, BLOCK, HEAD_SIZE))
    tile_scratch = pltpu.VMEM(tile.shape, BF16)
    score = (HEADS, BLOCK, 2 * BLOCK)
    pieces = call(
        d_out_body, [shape((BLOCK, HEAD_SIZE))] * HEADS, [tile_scratch],
        n_smem=1, n_vmem=4, flops=D_OUT_FLOPS, name="d_out",
    )(ids, out_grad, near, *far)
    pieces = [pieces[0]] + [ctx_swap(pieces[k], k * group) for k in range(1, HEADS)]
    if small:
        own, cross[0], *pieces = together(own, cross[0], *pieces)
    else:
        own, *pieces = together(own, *pieces)
    others = [ctx_swap(own, r) for r in range(1, group)]
    vmem = 16 if group == 2 else 40
    kv_scratch = pltpu.VMEM((group, HEADS, 2 * BLOCK, HEAD_SIZE), BF16)
    send, probs = call(
        functools.partial(forward_body, group),
        [tile, shape(score)],
        [kv_scratch, pltpu.VMEM(score, F32), pltpu.VMEM(score, BF16), tile_scratch, pltpu.SemaphoreType.DMA((2,))],
        n_smem=3, n_vmem=group, out_specs=[HBM] * 2, vmem=vmem, name="forward",
    )(ids, key_blocks, block_counts, own, *others)
    back = exchange(send)
    if small:
        same = [out_grad, ctx_swap(out_grad, 2)]
        cross.append(ctx_swap(same[1], 1))
        back, same[1], cross[1] = together(back, same[1], cross[1])
    dq, near_kv, *far_kv = call(
        functools.partial(backward_body, group),
        [tile, pair] + [tile] * (2 * group - 2),
        [
            tile_scratch, kv_scratch, tile_scratch, pltpu.VMEM(score, BF16), pltpu.VMEM(score, F32),
            pltpu.VMEM(score, BF16),
            pltpu.VMEM((group, HEADS, 2 * BLOCK, HEAD_SIZE), F32), pltpu.SemaphoreType.DMA((group + 2,)),
        ],
        n_smem=2, n_vmem=HEADS, n_hbm=group + 1, vmem=vmem, name="backward",
    )(ids, key_blocks, *pieces, own, *others, probs)
    arrived = [ctx_swap(part, i // 2 + 1) for i, part in enumerate(far_kv)]
    send = call(
        combine_body, shape((HEADS, 3 * BLOCK, HEAD_SIZE)), n_vmem=2 * group, vmem=vmem,
        name="combine",
    )(dq, near_kv, *arrived)
    back, send = together(back, send)
    grads = exchange(send)
    tokens = shape((1, BLOCK, HEADS * HEAD_SIZE))
    grad_queries, grad_keys, grad_values = call(unpack_body, [tokens] * 3, n_vmem=1, name="unpack")(grads)
    if small:
        mine, parts = reduce_weight(own_features(ids, back), [same[0], cross[0], same[1], cross[1]])
        mine, grad_queries, grad_keys, grad_values = together(
            mine, grad_queries, grad_keys, grad_values
        )
        grad_weight = mine + sum(part.astype(F32) for part in parts)
    else:
        grad_weight = lax.psum_scatter(
            dot(back.reshape(HEADS * HEAD_SIZE, BLOCK), out_grad[0], NN),
            ("dp", "ctx"), scatter_dimension=0, tiled=True,
        )
    output = call(
        output_body, shape((1, BLOCK, columns)), n_smem=1, n_vmem=4, vmem=60, name="output",
    )(ids, back, near, *far)
    return (output, grad_queries, grad_keys, grad_values, grad_weight)


def solution(mesh):
    tokens = P("dp", "ctx", None)
    return jax.shard_map(
        local,
        mesh=mesh,
        in_specs=(
            tokens, tokens, tokens, P("dp", None), tokens,
            P("dp", None, None, None), P("dp", None, None),
        ),
        out_specs=(tokens, tokens, tokens, tokens, P(("dp", "ctx"), None)),
        check_vma=False,
    )
```
